32 devices in a mesh: lev: 4 (over y, x), wav: 8 (over z, core).
Axes of the slice: x: 2, y: 2, z: 4, core: 2. Of those that a mesh axis runs over, the one named last changes fastest.
Arguments:
- grid_field: bfloat16 [128, 640, 1280], P('lev', 'wav'), may hold values from -6 to 6
- legendre: bfloat16 [640, 640, 640], P('wav'), may hold values from -0.25 to 0.25
- wave_of_slot: int32 [640], replicated, may hold values from 0 to 639, each once
- lat_of_row: int32 [640], P('wav'), may hold values from 0 to 639, each once
- analysis: bfloat16 [128, 128], replicated, may hold values from -0.5 to 0.5
- synthesis: bfloat16 [128, 128], replicated, may hold values from -0.5 to 0.5
- mode_rates: float32 [128], replicated, may hold values from 0.05 to 5
- flux_weights: float32 [128], replicated, may hold values from -0.5 to 0.5
- remap_mats: bfloat16 [4, 64, 128, 128], P('lev', 'wav'), may hold values from -0.5 to 0.5
- pair_dest: int32 [4, 64, 1], P('lev'), may hold values from 0 to 7; in each aligned block of 8 rows (0 to 7, 8 to 15, ..., all dimensions but the last counted through in order) at most 2 rows name the same one
- pair_src: int32 [4, 64], P('lev'), may hold values from 0 to 799
- pair_dst: int32 [4, 64], P('lev'), may hold values from 0 to 47
- ocean_temp: float32 [8, 192, 1024], P(None, 'lev', 'wav'), may hold values from -6 to 6
- diffusivity: float32 [192, 1024], P('lev', 'wav'), may hold values from 0.05 to 0.24
- surface_heat: float32 [192, 1024], P('lev', 'wav'), may hold values from -4 to 4
- land_mask: int32 [192, 1024], P('lev', 'wav'), may hold values 0 or 1
Outputs:
- atm_out: bfloat16 [128, 640, 1280], P('lev', 'wav')
- ocean_out: float32 [8, 192, 1024], P(None, 'lev', 'wav')
- ocean_flux: float32 [192, 1024], P('lev', 'wav')
The draws below stay inside these ranges and needn't reach their ends.
Inputs may be any that keep to these rules, and one draw needn't show every extreme that they name: `wave_of_slot`: each wavenumber names exactly one slot. `lat_of_row`: each latitude names exactly one row. `pair_dest`: within the pairs of one source owner (aligned blocks of 8 pairs of a level row) no destination column is named more than 2 times.
All inputs are finite; a program needn't handle non-finite values. No bound on the sum of `land_mask` on one device may be relied on, other than what follows from the above.
Results may differ from the reference program's by a relative error of at most 0.015.
Values may be sent and summed in bfloat16 or wider, within the bound.
No kernel may reach another device: no remote copies, remote signals or barrier semaphores. Data moves between devices by JAX's collectives and lax.ppermute only.
A program may use at most 192 MiB of HBM per device.

```python
import math
import jax
import jax.numpy as jnp
import numpy as np
from jax import lax

NLON = 1280
NLAT = 640
WAVES = 640
LEVELS = 128
OLEV = 8
OX = 48
OY = 128
CAP = 2
SWEEPS = 4
ASEG = 800
PAIRS_DEV = 8
PAIRS_ROW = 64
O_ROWS = 192
O_COLS = 1024
N_LEV = 4
N_WAV = 8


def place_ends(values, rng, least, top_value):
    spot = [jax.random.randint(jax.random.fold_in(rng, axis), (), 0, length) for axis, length in enumerate(values.shape)]
    main_axis = values.shape.index(max(values.shape))
    beside = spot[:main_axis] + [(spot[main_axis] + 1) % values.shape[main_axis]] + spot[main_axis + 1:]
    return values.at[tuple(spot)].set(least).at[tuple(beside)].set(top_value)


def levels(own_key, dims, split, low, top_value):
    loudness = 1.0
    for position, parts in split:
        draws = jax.random.uniform(jax.random.fold_in(jax.random.fold_in(own_key, 6), position), (parts,), jnp.float32, low / len(split), top_value / len(split))
        loudness = loudness * jnp.repeat(jnp.exp(draws), dims[position] // parts).reshape((-1,) + (1,) * (len(dims) - 1 - position))
    return loudness


def assign_block(own_key, own, number, rows, number_of, top, bound, skew):
    order = jax.random.permutation(own_key, number_of)
    heavy_load, common = shares(number_of, rows * top, bound, skew, True), shares(number_of, rows * top, bound, skew, False)
    places = jnp.arange(number_of)

    def named(sizes, rotation):
        used = int((sizes > 0).sum())
        fixed = max(1, used // 4)
        shifted = fixed + (places - fixed + rotation * (used - fixed)) % max(1, number_of - fixed)
        return jnp.zeros((number_of,), jnp.int32).at[order[jnp.where(places < fixed, places, shifted)]].set(jnp.asarray(sizes, jnp.int32))

    sizes = jnp.where(number % 4 == 0, named(heavy_load, number // 4), named(common, number - number // 4 - 1))
    mixed = jax.random.permutation(jax.random.fold_in(own, 3), number_of)
    giver, sink = mixed[0:number_of // 2 * 2:2], mixed[1:number_of // 2 * 2:2]
    margin = jnp.minimum(sizes[giver] - 1, bound - sizes[sink]) // 2
    margin = jnp.where((giver == order[0]) | (sink == order[0]) | (sizes[sink] == 0), 0, jnp.maximum(margin, 0))
    shifted = jax.random.randint(jax.random.fold_in(own, 4), (number_of // 2,), 0, 1 << 20) % (margin + 1)
    sizes = sizes.at[giver].add(-shifted).at[sink].add(shifted)
    members = jnp.searchsorted(jnp.cumsum(sizes), jnp.arange(rows * top), side="right").astype(jnp.int32)
    table = members.reshape(top, rows).T
    table = table[jax.random.permutation(jax.random.fold_in(own, 1), rows)]
    rotation = jax.random.randint(jax.random.fold_in(own, 2), (rows, 1), 0, top)
    return jnp.take_along_axis(table, (jnp.arange(top)[None, :] + rotation) % top, axis=1)


def shares(amount, total, most, skew, full):
    weights = [(1 << 20) // math.isqrt(rank ** skew) + 1 for rank in range(1, amount + 1)]
    largest = most if full else min(most, max(-(-total // amount), total * weights[0] // sum(weights)))
    least = 1 if total - largest >= amount - 1 else 0
    holding, surplus = [largest] + [least] * (amount - 1), total - largest - least * (amount - 1)
    while surplus > 0:
        movable = [i for i in range(1, amount) if holding[i] < largest] or [i for i in range(1, amount) if holding[i] < most]
        mass, left = sum([weights[i] for i in movable]), surplus
        for i in movable:
            addition = min(most - holding[i], max(1, left * weights[i] // mass), surplus)
            holding[i] = holding[i] + addition
            surplus = surplus - addition
    return np.array(holding)


def centred(rng, shape, scale, bound, pieces=(), kind=jnp.bfloat16):
    level = levels(rng, shape, pieces, -0.22, 0.18) if pieces else 1.0
    drawn = jax.random.normal(rng, shape, jnp.float32) * scale * level
    return jnp.minimum(jnp.maximum(drawn, -bound), bound).astype(kind)


def setup_inputs(seed: int = 0) -> dict:
    splits = jax.random.split(jax.random.key(seed), 17)
    grid_field = centred(splits[0], (LEVELS, NLAT, NLON), 1.0, 6.0, ((0, 4), (1, 8)))
    legendre = centred(splits[1], (WAVES, NLAT, WAVES), NLAT ** -0.5, 0.25, ((0, 8),))
    wave_of_slot = jax.random.permutation(splits[2], WAVES).astype(jnp.int32)
    lat_of_row = jax.random.permutation(splits[3], NLAT).astype(jnp.int32)
    analysis = centred(splits[4], (LEVELS, LEVELS), LEVELS ** -0.5, 0.5)
    synthesis = centred(splits[5], (LEVELS, LEVELS), LEVELS ** -0.5, 0.5)
    mode_rates = jnp.clip(jnp.exp(jax.random.uniform(splits[6], (LEVELS,), jnp.float32, math.log(0.05), math.log(5.0))), 0.05, 5.0)
    flux_weights = centred(splits[7], (LEVELS,), LEVELS ** -0.5, 0.5, (), jnp.float32)
    remap_mats = centred(splits[8], (N_LEV, PAIRS_ROW, OY, OY), OY ** -0.5, 0.5, ((0, 4), (1, 8)))
    pair_dest_keys = jax.random.split(jax.random.fold_in(splits[9], 1), N_LEV * PAIRS_ROW // PAIRS_DEV)
    pair_dest_turns = jax.random.permutation(jax.random.fold_in(splits[9], 3), N_LEV * PAIRS_ROW // PAIRS_DEV)
    pair_dest = jax.vmap(lambda own, number: assign_block(jax.random.fold_in(splits[9], 2), own, number, PAIRS_DEV, N_WAV, 1, CAP, 2))(pair_dest_keys, pair_dest_turns).reshape((N_LEV, PAIRS_ROW, 1))
    pair_src = place_ends(jax.random.randint(splits[10], (N_LEV, PAIRS_ROW), 0, ASEG), jax.random.fold_in(splits[10], 1), 0, ASEG - 1).astype(jnp.int32)
    pair_dst = place_ends(jax.random.randint(splits[11], (N_LEV, PAIRS_ROW), 0, OX), jax.random.fold_in(splits[11], 1), 0, OX - 1).astype(jnp.int32)
    ocean_temp = centred(splits[12], (OLEV, O_ROWS, O_COLS), 1.0, 6.0, ((1, 4), (2, 8)), jnp.float32)
    diffusivity = jnp.clip(0.05 + 0.19 * jax.random.uniform(splits[13], (O_ROWS, O_COLS), jnp.float32) ** levels(splits[13], (O_ROWS, O_COLS), ((0, 4), (1, 8)), -0.2, 0.2), 0.05, 0.24)
    surface_heat = centred(splits[14], (O_ROWS, O_COLS), 0.5, 4.0, ((0, 4), (1, 8)), jnp.float32)
    land_mask = place_ends((jax.random.randint(splits[15], (O_ROWS, O_COLS), 0, 4) < 3).astype(jnp.int32), jax.random.fold_in(splits[15], 1), 0, 1)
    return dict(grid_field=grid_field, legendre=legendre, wave_of_slot=wave_of_slot, lat_of_row=lat_of_row, analysis=analysis, synthesis=synthesis, mode_rates=mode_rates, flux_weights=flux_weights, remap_mats=remap_mats, pair_dest=pair_dest, pair_src=pair_src, pair_dst=pair_dst, ocean_temp=ocean_temp, diffusivity=diffusivity, surface_heat=surface_heat, land_mask=land_mask)


def column_table(wave_ids, halves, lon_count):
    longitude = jnp.arange(lon_count, dtype=jnp.int32)
    phases = longitude[:, None] * wave_ids[None, :] % lon_count
    angles = phases.astype(jnp.float32) * (2.0 * math.pi / lon_count)
    factor = math.sqrt(2.0 / lon_count)
    matrix = jnp.where(halves[None, :] == 0, factor * jnp.cos(angles), -factor * jnp.sin(angles))
    return matrix.astype(jnp.bfloat16)

def reference(grid_field, legendre, wave_of_slot, lat_of_row, analysis, synthesis, mode_rates, flux_weights, remap_mats, pair_dest, pair_src, pair_dst, ocean_temp, diffusivity, surface_heat, land_mask):
    positions = jnp.arange(2 * WAVES, dtype=jnp.int32)
    wave_matrix = column_table(jnp.repeat(wave_of_slot, 2), positions % 2, NLON)
    fourier = jnp.dot(grid_field.reshape(LEVELS * NLAT, NLON), wave_matrix, preferred_element_type=jnp.float32).astype(jnp.bfloat16)
    fourier = fourier.reshape(LEVELS, NLAT, WAVES, 2)
    degree = jnp.arange(WAVES, dtype=jnp.int32)
    damp_base = (degree * (degree + 1)).astype(jnp.float32) / (WAVES * WAVES)
    damping = 1.0 / (1.0 + mode_rates[:, None] * damp_base[None, :])
    analysis_wide = analysis.astype(jnp.float32)
    synthesis_wide = synthesis.astype(jnp.float32)

    def per_slot(slot_id):
        columns = lax.dynamic_index_in_dim(fourier, slot_id, 2, keepdims=False).astype(jnp.float32)
        legendre_slot = lax.dynamic_index_in_dim(legendre, slot_id, 0, keepdims=False).astype(jnp.float32)
        spectra = jnp.einsum('xrk,rn->kxn', columns, legendre_slot)
        retained = degree >= wave_of_slot[slot_id]
        spectra = jnp.where(retained[None, None, :], spectra, 0.0).astype(jnp.bfloat16)
        modal_coef = jnp.einsum('ix,kxn->kin', analysis_wide, spectra.astype(jnp.float32))
        modal_coef = (modal_coef * damping[None]).astype(jnp.bfloat16)
        solved = jnp.einsum('xi,kin->kxn', synthesis_wide, modal_coef.astype(jnp.float32)).astype(jnp.bfloat16)
        solved_wide = solved.astype(jnp.float32)
        flux_coef = jnp.einsum('x,kxn->kn', flux_weights, solved_wide).astype(jnp.bfloat16)
        grid_coef = jnp.einsum('rn,kxn->kxr', legendre_slot, solved_wide).astype(jnp.bfloat16)
        flux_lat = jnp.einsum('rn,kn->kr', legendre_slot, flux_coef.astype(jnp.float32)).astype(jnp.bfloat16)
        return (grid_coef, flux_lat)
    grid_coef, flux_lat = lax.map(per_slot, jnp.arange(WAVES, dtype=jnp.int32))
    coef_flat = grid_coef.reshape(2 * WAVES, LEVELS * NLAT)
    regridded = lax.dot_general(coef_flat, wave_matrix, (((0,), (1,)), ((), ())), preferred_element_type=jnp.float32)
    flux_flat = flux_lat.reshape(2 * WAVES, NLAT)
    flux_grid = lax.dot_general(flux_flat, wave_matrix, (((0,), (1,)), ((), ())), preferred_element_type=jnp.float32).astype(jnp.bfloat16)
    latitude = jnp.sin(math.pi * (lat_of_row.astype(jnp.float32) + 0.5) / NLAT - math.pi / 2)
    atm_out = (regridded.reshape(LEVELS, NLAT, NLON) * (1.0 + grid_field.astype(jnp.float32) * latitude[None, :, None])).astype(jnp.bfloat16)
    ocean_mask = land_mask.astype(jnp.float32)
    level_one = (jnp.arange(OLEV, dtype=jnp.int32) == 0).astype(jnp.float32)[:, None, None]
    ocean_now = ocean_temp * ocean_mask[None]
    for sweep_idx in range(SWEEPS):
        padded = jnp.pad(ocean_now, ((0, 0), (1, 1), (1, 1)))
        laplace = padded[:, 2:, 1:-1] + padded[:, :-2, 1:-1] + padded[:, 1:-1, 2:] + padded[:, 1:-1, :-2] - 4.0 * ocean_now
        ocean_now = ocean_mask[None] * (ocean_now + diffusivity[None] * laplace + level_one * surface_heat[None])
    segments = flux_grid.reshape(NLAT * (NLON // OY), OY)
    source = jnp.arange(PAIRS_ROW, dtype=jnp.int32) // PAIRS_DEV

    def per_row(row_data):
        row_mats, row_dest, row_src, row_dst = row_data
        chosen = segments[source * ASEG + row_src].astype(jnp.float32)
        products = jnp.einsum('pij,pj->pi', row_mats.astype(jnp.float32), chosen)
        target = row_dst * N_WAV + row_dest[:, 0]
        return jax.ops.segment_sum(products, target, num_segments=OX * N_WAV)
    rows_out = lax.map(per_row, (remap_mats, pair_dest, pair_src, pair_dst))
    ocean_flux = rows_out.reshape(N_LEV * OX, N_WAV * OY)
    return (atm_out, ocean_now, ocean_flux)
```

```python
import math

import jax
import jax.numpy as jnp
from jax import lax
from jax.sharding import PartitionSpec as P


SWEEPS = 4
CAP = 2
AXES = ("lev", "wav")
CHUNKS = (1, 2, 2)


def with_halo(value, sides, width):
    for axis, dim in sides:
        count, length = (lax.axis_size(axis), value.shape[dim])
        up = [(i, (i + 1) % count) for i in range(count - 1)]
        down = [(j, i) for i, j in up]
        last = lax.slice_in_dim(value, length - width, length, axis=dim)
        initial = lax.slice_in_dim(value, 0, width, axis=dim)
        before = lax.ppermute(last, axis, up)
        after = lax.ppermute(initial, axis, down)
        value = jnp.concatenate([before, value, after], axis=dim)
    return value


def exchange(value):
    return lax.all_to_all(value, AXES, split_axis=0, concat_axis=0, tiled=True)


def wave_table(waves, valid, lon_count):
    shape = waves.shape[:-1] + (2, waves.shape[-1])
    quarter = jnp.arange(2, dtype=jnp.int32) * (lon_count // 4)
    quarter = jnp.broadcast_to(quarter[:, None], shape).reshape(-1)
    waves = jnp.broadcast_to(waves[..., None, :], shape).reshape(-1)
    scale = jnp.where(valid, math.sqrt(2.0 / lon_count), 0.0)
    scale = jnp.broadcast_to(scale[..., None, :], shape).reshape(-1)
    longitude = jnp.arange(lon_count, dtype=jnp.int32)
    steps = (waves[:, None] * longitude[None, :] + quarter[:, None]).astype(jnp.float32)
    steps = steps - lon_count * jnp.round(steps * (1.0 / lon_count))
    return (scale[:, None] * jnp.cos(steps * (2.0 * math.pi / lon_count))).astype(jnp.bfloat16)


def return_order(steps):
    return list(range(1, steps)) + [0]


def split_slots(count):
    total = sum(CHUNKS)
    if count % total:
        return [(0, count)]
    unit, start, out = count // total, 0, []
    for part in CHUNKS:
        out.append((start, part * unit))
        start += part * unit
    return out


def ocean(ocean_temp, diffusivity, surface_heat, land_mask):
    ocean_levels = ocean_temp.shape[0]
    ocean_mask = land_mask.astype(jnp.float32)
    level_one = (jnp.arange(ocean_levels, dtype=jnp.int32) == 0).astype(jnp.float32)[:, None, None]
    ocean_now = ocean_temp * ocean_mask[None]
    stacked = jnp.concatenate(
        [ocean_now, ocean_mask[None], diffusivity[None], surface_heat[None]], axis=0
    )
    padded = with_halo(stacked.astype(jnp.bfloat16), (("lev", 1), ("wav", 2)), SWEEPS).astype(
        stacked.dtype
    )
    current = padded[:ocean_levels]
    for sweep_idx in range(SWEEPS):
        margin = sweep_idx + 1
        inside = current[:, 1:-1, 1:-1]
        laplace = (
            current[:, 2:, 1:-1]
            + current[:, :-2, 1:-1]
            + current[:, 1:-1, 2:]
            + current[:, 1:-1, :-2]
            - 4.0 * inside
        )
        mask_in = padded[ocean_levels, margin:-margin, margin:-margin]
        kappa_in = padded[ocean_levels + 1, margin:-margin, margin:-margin]
        heat_in = padded[ocean_levels + 2, margin:-margin, margin:-margin]
        current = mask_in[None] * (inside + kappa_in[None] * laplace + level_one * heat_in[None])
    return current


def per_device(
    grid_field,
    legendre,
    wave_of_slot,
    lat_of_row,
    analysis,
    synthesis,
    mode_rates,
    flux_weights,
    remap_mats,
    pair_dest,
    pair_src,
    pair_dst,
    ocean_temp,
    diffusivity,
    surface_heat,
    land_mask,
):
    groups = lax.axis_size("lev")
    owners = lax.axis_size("wav")
    devices = groups * owners
    my_group = lax.axis_index("lev")
    my_owner = lax.axis_index("wav")
    lev_dev, lat_dev, lon_count = grid_field.shape
    wave_count = wave_of_slot.shape[0]
    slots_owner = wave_count // owners
    slots_dev = -(-slots_owner // groups)
    cells = lev_dev * lat_dev
    rows_flat = grid_field.reshape(cells, lon_count)
    degree = jnp.arange(wave_count, dtype=jnp.int32)
    damp_base = (degree * (degree + 1)).astype(jnp.float32) / float(wave_count * wave_count)
    damping = 1.0 / (1.0 + mode_rates[:, None] * damp_base[None, :])

    def slots_of(group, owner, start, count):
        local = group * slots_dev + start + jnp.arange(count, dtype=jnp.int32)
        slot = owner * slots_owner + jnp.minimum(local, slots_owner - 1)
        return local, wave_of_slot[slot], local < slots_owner

    chunks = split_slots(slots_dev)
    spare = groups * slots_dev - slots_owner
    all_waves = jnp.pad(wave_of_slot.reshape(owners, slots_owner), ((0, 0), (0, spare)))
    all_waves = all_waves.reshape(owners, groups, slots_dev).transpose(1, 0, 2)
    all_valid = jnp.arange(groups * slots_dev, dtype=jnp.int32) < slots_owner
    all_valid = all_valid.reshape(groups, 1, slots_dev)

    def forward(start, count):
        waves = all_waves[:, :, start : start + count]
        valid = jnp.broadcast_to(all_valid[:, :, start : start + count], waves.shape)
        table = lax.optimization_barrier(wave_table(waves, valid, lon_count))
        fourier = lax.dot_general(
            table, rows_flat, (((1,), (1,)), ((), ())), preferred_element_type=jnp.float32
        ).astype(jnp.bfloat16)
        return table, fourier.reshape(devices, 2 * count, cells)

    def spectral(arrived, start, count):
        arrived, my_analysis, my_synthesis, my_damping, my_weights = lax.optimization_barrier(
            (arrived, analysis, synthesis, damping, flux_weights)
        )
        local, my_waves, _ = slots_of(my_group, my_owner, start, count)
        if slots_owner == slots_dev * groups:
            leg = lax.dynamic_slice_in_dim(legendre, my_group * slots_dev + start, count, axis=0)
        else:
            leg = jnp.take(legendre, jnp.minimum(local, slots_owner - 1), axis=0)
        fields = arrived.reshape(groups, owners, 2, count, lev_dev, lat_dev)
        fields = fields.transpose(3, 1, 2, 0, 4, 5).reshape(
            count, owners, 2 * groups * lev_dev, lat_dev
        )
        leg_rows = leg.reshape(count, owners, lat_dev, wave_count)
        spectra = jnp.einsum(
            "swmr,swrn->smn", fields, leg_rows, preferred_element_type=jnp.float32
        ).reshape(count, 2, groups * lev_dev, wave_count)
        retained = degree[None, :] >= my_waves[:, None]
        spectra = jnp.where(retained[:, None, None, :], spectra, 0.0).astype(jnp.bfloat16)
        modal_coef = jnp.einsum(
            "ix,skxn->skin", my_analysis, spectra, preferred_element_type=jnp.float32
        )
        modal_coef = (modal_coef * my_damping[None, None]).astype(jnp.bfloat16)
        solved = jnp.einsum(
            "xi,skin->skxn", my_synthesis, modal_coef, preferred_element_type=jnp.float32
        ).astype(jnp.bfloat16)
        flux_coef = jnp.sum(
            my_weights[None, None, :, None] * solved.astype(jnp.float32), axis=2
        ).astype(jnp.bfloat16)
        grid_coef = jnp.einsum(
            "smn,swrn->swmr",
            solved.reshape(count, 2 * groups * lev_dev, wave_count),
            leg_rows,
            preferred_element_type=jnp.float32,
        ).astype(jnp.bfloat16)
        grid_coef = grid_coef.reshape(count, owners, 2, groups, lev_dev, lat_dev)
        grid_coef = grid_coef.transpose(3, 1, 2, 0, 4, 5).reshape(devices, 2 * count, cells)
        flux_lat = lax.dot_general(
            flux_coef, leg, (((2,), (2,)), ((0,), (0,))), preferred_element_type=jnp.float32
        ).astype(jnp.bfloat16)
        flux_lat = flux_lat.reshape(count, 2, owners, lat_dev).transpose(1, 0, 2, 3)
        return grid_coef, flux_lat.reshape(2 * count, owners, lat_dev)

    tables, arrivals, returned, sent, flux_parts = [], [], [], [], []
    for chunk in chunks:
        table, fourier = forward(*chunk)
        tables.append(table)
        arrivals.append(exchange(fourier))
    for index, chunk in enumerate(chunks):
        grid_coef, flux_lat = spectral(arrivals[index], *chunk)
        sent.append(grid_coef)
        flux_parts.append(flux_lat)
    for value in sent:
        returned.append(exchange(value))
    flux_lat = jnp.concatenate(flux_parts, axis=0).transpose(1, 0, 2)
    flux_copies = jnp.broadcast_to(flux_lat[None], (groups,) + flux_lat.shape)
    flux_back = exchange(flux_copies.reshape(devices, 2 * slots_dev, lat_dev))

    flux_grid = 0.0
    for (start, count), table in zip(chunks, tables):
        part = flux_back[:, 2 * start : 2 * (start + count)].reshape(-1, lat_dev)
        flux_grid += lax.dot_general(
            part, table, (((0,), (0,)), ((), ())), preferred_element_type=jnp.float32
        )
    flux_grid = flux_grid.astype(jnp.bfloat16)

    latitude = jnp.sin(
        math.pi * (lat_of_row.astype(jnp.float32) + 0.5) / (lat_dev * owners) - math.pi / 2
    )
    latitude = jnp.broadcast_to(latitude[None], (lev_dev, lat_dev)).reshape(cells, 1)
    regridded = 0.0
    for index in return_order(len(chunks)):
        regridded += lax.dot_general(
            returned[index].reshape(-1, cells),
            tables[index],
            (((0,), (0,)), ((), ())),
            preferred_element_type=jnp.float32,
        )
    atm_out = regridded * (1.0 + rows_flat.astype(jnp.float32) * latitude)
    atm_out = atm_out.astype(jnp.bfloat16).reshape(lev_dev, lat_dev, lon_count)

    ocean_now = ocean(ocean_temp, diffusivity, surface_heat, land_mask)

    ocean_rows, ocean_cols = diffusivity.shape
    pieces = lon_count // ocean_cols
    segments = flux_grid.reshape(lat_dev * pieces, ocean_cols)
    pairs_dev = remap_mats.shape[1]
    all_dest = pair_dest[0, :, 0].reshape(owners, pairs_dev)
    all_dst = pair_dst[0].reshape(owners, pairs_dev)
    earlier = jnp.arange(pairs_dev)[None, :] < jnp.arange(pairs_dev)[:, None]
    rank = jnp.sum(
        (all_dest[:, :, None] == all_dest[:, None, :]) & earlier[None], axis=2, dtype=jnp.int32
    )
    my_src = lax.dynamic_slice_in_dim(pair_src[0], my_owner * pairs_dev, pairs_dev)
    chosen = jnp.take(segments, my_src, axis=0)
    products = jnp.einsum("pij,pj->pi", remap_mats[0], chosen, preferred_element_type=jnp.float32)
    place = lax.dynamic_index_in_dim(all_dest * CAP + rank, my_owner, 0, keepdims=False)
    outgoing = jnp.dot(
        (jnp.arange(owners * CAP, dtype=jnp.int32)[:, None] == place[None, :]).astype(jnp.float32),
        products,
        precision=lax.Precision.HIGHEST,
        preferred_element_type=jnp.float32,
    )
    outgoing = outgoing.reshape(owners, CAP, ocean_cols)
    incoming = lax.all_to_all(outgoing, "wav", split_axis=0, concat_axis=0, tiled=True)
    mine = (all_dest == my_owner)[:, None, :] & (
        rank[:, None, :] == jnp.arange(CAP, dtype=jnp.int32)[None, :, None]
    )
    row_hit = all_dst[None, :, None, :] == jnp.arange(ocean_rows, dtype=jnp.int32)[:, None, None, None]
    picker = jnp.any(mine[None] & row_hit, axis=3).astype(jnp.float32)
    ocean_flux = jnp.dot(
        picker.reshape(ocean_rows, owners * CAP),
        incoming.reshape(owners * CAP, ocean_cols),
        precision=lax.Precision.HIGHEST,
        preferred_element_type=jnp.float32,
    )
    return (atm_out, ocean_now, ocean_flux)


def solution(mesh):
    return jax.shard_map(
        per_device,
        mesh=mesh,
        in_specs=(
            P("lev", "wav", None),
            P("wav", None, None),
            P(),
            P("wav"),
            P(),
            P(),
            P(),
            P(),
            P("lev", "wav", None, None),
            P("lev", None, None),
            P("lev", None),
            P("lev", None),
            P(None, "lev", "wav"),
            P("lev", "wav"),
            P("lev", "wav"),
            P("lev", "wav"),
        ),
        out_specs=(P("lev", "wav", None), P(None, "lev", "wav"), P("lev", "wav")),
        check_vma=False,
    )
```

```python
import functools
import math

import jax
import jax.numpy as jnp
from jax import lax
from jax.experimental import pallas as pl
from jax.experimental.pallas import tpu as pltpu
from jax.sharding import PartitionSpec as P


SWEEPS = 4
CAP = 2
AXES = ("lev", "wav")
CHUNKS = (2, 3)
UNIT = 4
LANES = 128


def with_halo(value, sides, width):
    for axis, dim in sides:
        count, length = (lax.axis_size(axis), value.shape[dim])
        up = [(i, (i + 1) % count) for i in range(count - 1)]
        down = [(j, i) for i, j in up]
        last = lax.slice_in_dim(value, length - width, length, axis=dim)
        initial = lax.slice_in_dim(value, 0, width, axis=dim)
        before = lax.ppermute(last, axis, up)
        after = lax.ppermute(initial, axis, down)
        value = jnp.concatenate([before, value, after], axis=dim)
    return value


def exchange(value):
    return lax.all_to_all(value, AXES, split_axis=0, concat_axis=0, tiled=True)


def table_kernel(unit, lon_count, waves_ref, table_ref):
    rows = waves_ref.shape[0]
    lane = lax.broadcasted_iota(jnp.int32, (rows, LANES), 1)
    half = (lax.broadcasted_iota(jnp.int32, (rows, LANES), 0) // unit) % 2
    waves = jnp.broadcast_to(waves_ref[...], (rows, LANES))
    scale = jnp.where(waves < 0, 0.0, math.sqrt(2.0 / lon_count))

    def angle(steps):
        steps = steps.astype(jnp.float32)
        steps = steps - lon_count * jnp.round(steps * (1.0 / lon_count))
        return steps * (2.0 * math.pi / lon_count)

    low = angle(waves * lane + half * (lon_count // 4))
    high = angle(waves * (lane * LANES))
    cos_low, sin_low = scale * jnp.cos(low), scale * jnp.sin(low)
    cos_high, sin_high = jnp.cos(high), jnp.sin(high)
    for tile in range(lon_count // LANES):
        part = cos_low * cos_high[:, tile : tile + 1] - sin_low * sin_high[:, tile : tile + 1]
        table_ref[:, tile * LANES : (tile + 1) * LANES] = part.astype(jnp.bfloat16)


def wave_table(waves, valid, unit, lon_count):
    devices, count = waves.shape
    waves = jnp.where(valid, waves, -1).reshape(devices, count // unit, 1, unit)
    waves = jnp.broadcast_to(waves, (devices, count // unit, 2, unit)).reshape(-1, 1)
    rows = waves.shape[0]
    block = math.gcd(rows, 128)
    if block % (2 * unit):
        block = rows
    return pl.pallas_call(
        functools.partial(table_kernel, unit, lon_count),
        grid=(rows // block,),
        in_specs=[pl.BlockSpec((block, 1), lambda i: (i, 0))],
        out_specs=pl.BlockSpec((block, lon_count), lambda i: (i, 0)),
        out_shape=jax.ShapeDtypeStruct((rows, lon_count), jnp.bfloat16),
    )(waves)


def segments(length, source, target):
    cuts = {0}
    cuts.update(i for i in range(1, length) if (source + i) % LANES == 0)
    cuts.update(i for i in range(1, length) if (target + i) % LANES == 0)
    return [
        ((source + i) // LANES, (target + i) // LANES, (target + i) % LANES) for i in sorted(cuts)
    ]


def move_runs(load, store, lane, runs):
    tile, value = 0, None
    for index, source, target, length in runs:
        for src, dst, low in segments(length, source, target):
            piece = pltpu.roll(load(index, src), (target - source) % LANES, 1) if (
                target - source
            ) % LANES else load(index, src)
            if dst != tile:
                store(tile, value)
                tile, value = dst, None
            value = piece if low == 0 else jnp.where(lane >= low, piece, value)
    store(tile, value)


def spectral_kernel(
    groups,
    owners,
    lev_dev,
    lat_dev,
    base_ref,
    waves_ref,
    arrived_ref,
    leg_ref,
    analysis_ref,
    synthesis_ref,
    damping_ref,
    weights_ref,
    sent_ref,
    flux_ref,
    stage_ref,
):
    rows = 2 * UNIT
    levels = groups * lev_dev
    wave_count = leg_ref.shape[2]
    width = owners * lat_dev
    unit = pl.program_id(0)
    lane = lax.broadcasted_iota(jnp.int32, (rows, LANES), 1)

    def take(group, carry):
        for x in range(lev_dev):
            first = pl.multiple_of((group * lev_dev + x) * rows, rows)

            def load(owner, tile):
                part = arrived_ref[group * owners + owner, :, tile * LANES : (tile + 1) * LANES]
                return part.astype(jnp.float32)

            def store(tile, value):
                stage_ref[tile, pl.ds(first, rows), :] = value

            move_runs(
                load,
                store,
                lane,
                [(w, x * lat_dev, w * lat_dev, lat_dev) for w in range(owners)],
            )
        return carry

    lax.fori_loop(0, groups, take, 0)
    degree = lax.broadcasted_iota(jnp.int32, (2 * levels, wave_count), 1)
    flux_row = lax.broadcasted_iota(jnp.int32, (16, wave_count), 0)

    def solve(slot, carry):
        halves = [
            [
                stage_ref[tile, pl.ds(k * UNIT + slot, levels, stride=rows), :]
                for tile in range(width // LANES)
            ]
            for k in range(2)
        ]
        fields = jnp.concatenate([jnp.concatenate(half, axis=1) for half in halves], axis=0)
        leg = leg_ref[slot]
        spectra = jnp.dot(fields.astype(jnp.bfloat16), leg, preferred_element_type=jnp.float32)
        wave = waves_ref[unit * UNIT + slot]
        spectra = jnp.where(degree >= wave, spectra, 0.0).astype(jnp.bfloat16)
        solved, flux = [], 0.0
        for k in range(2):
            modal = jnp.dot(
                analysis_ref[...],
                spectra[k * levels : (k + 1) * levels],
                preferred_element_type=jnp.float32,
            )
            modal = (modal * damping_ref[...]).astype(jnp.bfloat16)
            part = jnp.dot(
                synthesis_ref[...], modal, preferred_element_type=jnp.float32
            ).astype(jnp.bfloat16)
            coef = jnp.sum(weights_ref[...] * part.astype(jnp.float32), axis=0, keepdims=True)
            flux = jnp.where(flux_row == k, coef, flux)
            solved.append(part)
        solved.append(flux.astype(jnp.bfloat16))
        grid = lax.dot_general(
            jnp.concatenate(solved, axis=0),
            leg,
            (((1,), (1,)), ((), ())),
            preferred_element_type=jnp.float32,
        )
        for k in range(2):
            for tile in range(width // LANES):
                stage_ref[tile, pl.ds(k * UNIT + slot, levels, stride=rows), :] = grid[
                    k * levels : (k + 1) * levels, tile * LANES : (tile + 1) * LANES
                ]
            flux_ref[0, pl.ds(k * UNIT + slot, 1), :] = grid[2 * levels + k : 2 * levels + k + 1]
        return carry

    lax.fori_loop(0, UNIT, solve, 0)

    def send(group, carry):
        for w in range(owners):

            def load(x, tile):
                first = pl.multiple_of((group * lev_dev + x) * rows, rows)
                return stage_ref[tile, pl.ds(first, rows), :]

            def store(tile, value):
                sent_ref[group * owners + w, :, tile * LANES : (tile + 1) * LANES] = value.astype(
                    jnp.bfloat16
                )

            move_runs(
                load,
                store,
                lane,
                [(x, w * lat_dev, x * lat_dev, lat_dev) for x in range(lev_dev)],
            )
        return carry

    lax.fori_loop(0, groups, send, 0)


def spectral_call(
    arrived,
    legendre,
    base,
    waves,
    analysis,
    synthesis,
    damping,
    weights,
    groups,
    owners,
    lev_dev,
    lat_dev,
):
    devices, columns, cells = arrived.shape
    units = columns // (2 * UNIT)
    levels = groups * lev_dev
    rows_all, wave_count = legendre.shape[1:]
    body = functools.partial(spectral_kernel, groups, owners, lev_dev, lat_dev)
    whole = lambda shape: pl.BlockSpec(shape, lambda i, base, waves: (0,) * len(shape))
    return pl.pallas_call(
        body,
        grid_spec=pltpu.PrefetchScalarGridSpec(
            num_scalar_prefetch=2,
            grid=(units,),
            in_specs=[
                pl.BlockSpec((devices, 2 * UNIT, cells), lambda i, base, waves: (0, i, 0)),
                pl.BlockSpec(
                    (UNIT, rows_all, wave_count), lambda i, base, waves: (base[0] + i, 0, 0)
                ),
                whole(analysis.shape),
                whole(synthesis.shape),
                whole(damping.shape),
                whole((levels, 1)),
            ],
            out_specs=[
                pl.BlockSpec((devices, 2 * UNIT, cells), lambda i, base, waves: (0, i, 0)),
                pl.BlockSpec((1, 2 * UNIT, rows_all), lambda i, base, waves: (i, 0, 0)),
            ],
            scratch_shapes=[
                pltpu.VMEM((rows_all // LANES, levels * 2 * UNIT, LANES), jnp.float32)
            ],
        ),
        out_shape=[
            jax.ShapeDtypeStruct(arrived.shape, jnp.bfloat16),
            jax.ShapeDtypeStruct((units, 2 * UNIT, rows_all), jnp.float32),
        ],
        compiler_params=pltpu.CompilerParams(vmem_limit_bytes=48 * 1024 * 1024),
    )(base, waves, arrived, legendre, analysis, synthesis, damping, weights.reshape(levels, 1))


def split_slots(count, unit):
    total = sum(CHUNKS) * unit
    if count % total:
        return [(0, count)]
    start, out = 0, []
    for part in CHUNKS:
        part = count // sum(CHUNKS) * part
        out.append((start, part))
        start += part
    return out


def ocean(ocean_temp, diffusivity, surface_heat, land_mask):
    ocean_levels = ocean_temp.shape[0]
    ocean_mask = land_mask.astype(jnp.float32)
    level_one = (jnp.arange(ocean_levels, dtype=jnp.int32) == 0).astype(jnp.float32)[:, None, None]
    ocean_now = ocean_temp * ocean_mask[None]
    stacked = jnp.concatenate(
        [ocean_now, ocean_mask[None], diffusivity[None], surface_heat[None]], axis=0
    )
    padded = with_halo(stacked.astype(jnp.bfloat16), (("lev", 1), ("wav", 2)), SWEEPS).astype(
        stacked.dtype
    )
    current = padded[:ocean_levels]
    for sweep_idx in range(SWEEPS):
        margin = sweep_idx + 1
        inside = current[:, 1:-1, 1:-1]
        laplace = (
            current[:, 2:, 1:-1]
            + current[:, :-2, 1:-1]
            + current[:, 1:-1, 2:]
            + current[:, 1:-1, :-2]
            - 4.0 * inside
        )
        mask_in = padded[ocean_levels, margin:-margin, margin:-margin]
        kappa_in = padded[ocean_levels + 1, margin:-margin, margin:-margin]
        heat_in = padded[ocean_levels + 2, margin:-margin, margin:-margin]
        current = mask_in[None] * (inside + kappa_in[None] * laplace + level_one * heat_in[None])
    return current


def per_device(
    grid_field,
    legendre,
    wave_of_slot,
    lat_of_row,
    analysis,
    synthesis,
    mode_rates,
    flux_weights,
    remap_mats,
    pair_dest,
    pair_src,
    pair_dst,
    ocean_temp,
    diffusivity,
    surface_heat,
    land_mask,
):
    groups = lax.axis_size("lev")
    owners = lax.axis_size("wav")
    devices = groups * owners
    my_group = lax.axis_index("lev")
    my_owner = lax.axis_index("wav")
    lev_dev, lat_dev, lon_count = grid_field.shape
    wave_count = wave_of_slot.shape[0]
    slots_owner = wave_count // owners
    slots_dev = -(-slots_owner // groups)
    cells = lev_dev * lat_dev
    rows_flat = grid_field.reshape(cells, lon_count)
    degree = jnp.arange(wave_count, dtype=jnp.int32)
    damp_base = (degree * (degree + 1)).astype(jnp.float32) / float(wave_count * wave_count)
    damping = 1.0 / (1.0 + mode_rates[:, None] * damp_base[None, :])

    def slots_of(group, owner, start, count):
        local = group * slots_dev + start + jnp.arange(count, dtype=jnp.int32)
        slot = owner * slots_owner + jnp.minimum(local, slots_owner - 1)
        return local, wave_of_slot[slot], local < slots_owner

    exact = slots_owner == slots_dev * groups
    fused = (
        exact
        and slots_dev % UNIT == 0
        and lon_count % LANES == 0
        and cells % LANES == 0
        and owners * lat_dev % LANES == 0
        and groups * lev_dev % 8 == 0
    )
    unit = UNIT if fused else slots_dev
    chunks = split_slots(slots_dev, unit)
    spare = groups * slots_dev - slots_owner
    all_waves = jnp.pad(wave_of_slot.reshape(owners, slots_owner), ((0, 0), (0, spare)))
    all_waves = all_waves.reshape(owners, groups, slots_dev).transpose(1, 0, 2)
    all_valid = jnp.arange(groups * slots_dev, dtype=jnp.int32) < slots_owner
    all_valid = jnp.broadcast_to(all_valid.reshape(groups, 1, slots_dev), all_waves.shape)
    all_waves = all_waves.reshape(devices, slots_dev)
    all_valid = all_valid.reshape(devices, slots_dev)

    def forward(start, count):
        chosen = slice(start, start + count)
        table = wave_table(all_waves[:, chosen], all_valid[:, chosen], unit, lon_count)
        fourier = lax.dot_general(
            table, rows_flat, (((1,), (1,)), ((), ())), preferred_element_type=jnp.float32
        ).astype(jnp.bfloat16)
        return table, fourier.reshape(devices, 2 * count, cells)

    def spectral_fused(arrived, start, count):
        base = my_group * (slots_dev // UNIT) + start // UNIT
        first = my_owner * slots_owner + my_group * slots_dev + start
        my_waves = lax.dynamic_slice_in_dim(wave_of_slot, first, count)
        grid_coef, flux_lat = spectral_call(
            arrived,
            legendre,
            base.astype(jnp.int32).reshape(1),
            my_waves,
            analysis,
            synthesis,
            damping,
            flux_weights,
            groups,
            owners,
            lev_dev,
            lat_dev,
        )
        return grid_coef, flux_lat.astype(jnp.bfloat16).reshape(2 * count, owners, lat_dev)

    def spectral(arrived, start, count):
        arrived, my_analysis, my_synthesis, my_damping, my_weights = lax.optimization_barrier(
            (arrived, analysis, synthesis, damping, flux_weights)
        )
        local, my_waves, _ = slots_of(my_group, my_owner, start, count)
        if exact:
            leg = lax.dynamic_slice_in_dim(legendre, my_group * slots_dev + start, count, axis=0)
        else:
            leg = jnp.take(legendre, jnp.minimum(local, slots_owner - 1), axis=0)
        fields = arrived.reshape(groups, owners, 2, count, lev_dev, lat_dev)
        fields = fields.transpose(3, 1, 2, 0, 4, 5).reshape(
            count, owners, 2 * groups * lev_dev, lat_dev
        )
        leg_rows = leg.reshape(count, owners, lat_dev, wave_count)
        spectra = jnp.einsum(
            "swmr,swrn->smn", fields, leg_rows, preferred_element_type=jnp.float32
        ).reshape(count, 2, groups * lev_dev, wave_count)
        retained = degree[None, :] >= my_waves[:, None]
        spectra = jnp.where(retained[:, None, None, :], spectra, 0.0).astype(jnp.bfloat16)
        modal_coef = jnp.einsum(
            "ix,skxn->skin", my_analysis, spectra, preferred_element_type=jnp.float32
        )
        modal_coef = (modal_coef * my_damping[None, None]).astype(jnp.bfloat16)
        solved = jnp.einsum(
            "xi,skin->skxn", my_synthesis, modal_coef, preferred_element_type=jnp.float32
        ).astype(jnp.bfloat16)
        flux_coef = jnp.sum(
            my_weights[None, None, :, None] * solved.astype(jnp.float32), axis=2
        ).astype(jnp.bfloat16)
        grid_coef = jnp.einsum(
            "smn,swrn->swmr",
            solved.reshape(count, 2 * groups * lev_dev, wave_count),
            leg_rows,
            preferred_element_type=jnp.float32,
        ).astype(jnp.bfloat16)
        grid_coef = grid_coef.reshape(count, owners, 2, groups, lev_dev, lat_dev)
        grid_coef = grid_coef.transpose(3, 1, 2, 0, 4, 5).reshape(devices, 2 * count, cells)
        flux_lat = lax.dot_general(
            flux_coef, leg, (((2,), (2,)), ((0,), (0,))), preferred_element_type=jnp.float32
        ).astype(jnp.bfloat16)
        flux_lat = flux_lat.reshape(count, 2, owners, lat_dev).transpose(1, 0, 2, 3)
        return grid_coef, flux_lat.reshape(2 * count, owners, lat_dev)

    tables, arrivals, returned, sent, flux_parts = [], [], [], [], []
    for chunk in chunks:
        table, fourier = forward(*chunk)
        tables.append(table)
        arrivals.append(exchange(fourier))
    for index, chunk in enumerate(chunks):
        step = spectral_fused if fused else spectral
        grid_coef, flux_lat = step(arrivals[index], *chunk)
        sent.append(grid_coef)
        flux_parts.append(flux_lat)
    for value in sent:
        returned.append(exchange(value))
    flux_lat = jnp.concatenate(flux_parts, axis=0).transpose(1, 0, 2)
    flux_copies = jnp.broadcast_to(flux_lat[None], (groups,) + flux_lat.shape)
    flux_back = exchange(flux_copies.reshape(devices, 2 * slots_dev, lat_dev))

    flux_grid = 0.0
    for (start, count), table in zip(chunks, tables):
        part = flux_back[:, 2 * start : 2 * (start + count)].reshape(-1, lat_dev)
        flux_grid += lax.dot_general(
            part, table, (((0,), (0,)), ((), ())), preferred_element_type=jnp.float32
        )
    flux_grid = flux_grid.astype(jnp.bfloat16)

    latitude = jnp.sin(
        math.pi * (lat_of_row.astype(jnp.float32) + 0.5) / (lat_dev * owners) - math.pi / 2
    )
    latitude = jnp.broadcast_to(latitude[None], (lev_dev, lat_dev)).reshape(cells, 1)
    regridded = 0.0
    for index in range(len(chunks)):
        regridded += lax.dot_general(
            returned[index].reshape(-1, cells),
            tables[index],
            (((0,), (0,)), ((), ())),
            preferred_element_type=jnp.float32,
        )
        if index + 1 < len(chunks):
            regridded = lax.optimization_barrier(regridded)
    atm_out = regridded * (1.0 + rows_flat.astype(jnp.float32) * latitude)
    atm_out = atm_out.astype(jnp.bfloat16).reshape(lev_dev, lat_dev, lon_count)

    ocean_now = ocean(ocean_temp, diffusivity, surface_heat, land_mask)

    ocean_rows, ocean_cols = diffusivity.shape
    pieces = lon_count // ocean_cols
    segments = flux_grid.reshape(lat_dev * pieces, ocean_cols)
    pairs_dev = remap_mats.shape[1]
    all_dest = pair_dest[0, :, 0].reshape(owners, pairs_dev)
    all_dst = pair_dst[0].reshape(owners, pairs_dev)
    earlier = jnp.arange(pairs_dev)[None, :] < jnp.arange(pairs_dev)[:, None]
    rank = jnp.sum(
        (all_dest[:, :, None] == all_dest[:, None, :]) & earlier[None], axis=2, dtype=jnp.int32
    )
    my_src = lax.dynamic_slice_in_dim(pair_src[0], my_owner * pairs_dev, pairs_dev)
    chosen = jnp.take(segments, my_src, axis=0)
    products = jnp.einsum("pij,pj->pi", remap_mats[0], chosen, preferred_element_type=jnp.float32)
    place = lax.dynamic_index_in_dim(all_dest * CAP + rank, my_owner, 0, keepdims=False)
    outgoing = jnp.dot(
        (jnp.arange(owners * CAP, dtype=jnp.int32)[:, None] == place[None, :]).astype(jnp.float32),
        products,
        precision=lax.Precision.HIGHEST,
        preferred_element_type=jnp.float32,
    )
    outgoing = outgoing.reshape(owners, CAP, ocean_cols)
    incoming = lax.all_to_all(outgoing, "wav", split_axis=0, concat_axis=0, tiled=True)
    mine = (all_dest == my_owner)[:, None, :] & (
        rank[:, None, :] == jnp.arange(CAP, dtype=jnp.int32)[None, :, None]
    )
    row_hit = all_dst[None, :, None, :] == jnp.arange(ocean_rows, dtype=jnp.int32)[:, None, None, None]
    picker = jnp.any(mine[None] & row_hit, axis=3).astype(jnp.float32)
    ocean_flux = jnp.dot(
        picker.reshape(ocean_rows, owners * CAP),
        incoming.reshape(owners * CAP, ocean_cols),
        precision=lax.Precision.HIGHEST,
        preferred_element_type=jnp.float32,
    )
    return (atm_out, ocean_now, ocean_flux)


def solution(mesh):
    return jax.shard_map(
        per_device,
        mesh=mesh,
        in_specs=(
            P("lev", "wav", None),
            P("wav", None, None),
            P(),
            P("wav"),
            P(),
            P(),
            P(),
            P(),
            P("lev", "wav", None, None),
            P("lev", None, None),
            P("lev", None),
            P("lev", None),
            P(None, "lev", "wav"),
            P("lev", "wav"),
            P("lev", "wav"),
            P("lev", "wav"),
        ),
        out_specs=(P("lev", "wav", None), P(None, "lev", "wav"), P("lev", "wav")),
        check_vma=False,
    )
```

```python
import functools
import math

import jax
import jax.numpy as jnp
from jax import lax
from jax.experimental import pallas as pl
from jax.experimental.pallas import tpu as pltpu
from jax.sharding import PartitionSpec as P


SWEEPS = 4
CAP = 2
AXES = ("lev", "wav")
CHUNKS = (3, 2)
UNIT = 4
BLOCK = 1280
LANES = 128


def with_halo(value, sides, width):
    for axis, dim in sides:
        count, length = (lax.axis_size(axis), value.shape[dim])
        up = [(i, (i + 1) % count) for i in range(count - 1)]
        down = [(j, i) for i, j in up]
        last = lax.slice_in_dim(value, length - width, length, axis=dim)
        initial = lax.slice_in_dim(value, 0, width, axis=dim)
        before = lax.ppermute(last, axis, up)
        after = lax.ppermute(initial, axis, down)
        value = jnp.concatenate([before, value, after], axis=dim)
    return value


def exchange(value):
    return lax.all_to_all(value, AXES, split_axis=0, concat_axis=0, tiled=True)


def table_kernel(unit, lon_count, waves_ref, table_ref):
    rows = waves_ref.shape[0]
    lane = lax.broadcasted_iota(jnp.int32, (rows, LANES), 1)
    half = (lax.broadcasted_iota(jnp.int32, (rows, LANES), 0) // unit) % 2
    waves = jnp.broadcast_to(waves_ref[...], (rows, LANES))
    scale = jnp.where(waves < 0, 0.0, math.sqrt(2.0 / lon_count))

    def angle(steps):
        steps = steps.astype(jnp.float32)
        steps = steps - lon_count * jnp.round(steps * (1.0 / lon_count))
        return steps * (2.0 * math.pi / lon_count)

    low = angle(waves * lane + half * (lon_count // 4))
    high = angle(waves * (lane * LANES))
    cos_low, sin_low = scale * jnp.cos(low), scale * jnp.sin(low)
    cos_high, sin_high = jnp.cos(high), jnp.sin(high)
    for tile in range(lon_count // LANES):
        part = cos_low * cos_high[:, tile : tile + 1] - sin_low * sin_high[:, tile : tile + 1]
        table_ref[:, tile * LANES : (tile + 1) * LANES] = part.astype(jnp.bfloat16)


def swap(value, axis, bit, place):
    pairs = [(i, i ^ bit) for i in range(lax.axis_size(axis))]
    mine = (lax.axis_index(axis) // bit) % 2
    if place is None:
        kept = sent = value
        place = 1
    else:
        kept = lax.dynamic_index_in_dim(value, mine, place, keepdims=False)
        sent = lax.dynamic_index_in_dim(value, 1 - mine, place, keepdims=False)
    came = lax.ppermute(sent, axis, pairs)
    first = jnp.where(mine == 0, kept, came)
    second = jnp.where(mine == 0, came, kept)
    return jnp.stack([first, second], axis=place)


def bits_of(axis):
    return [1 << i for i in range(lax.axis_size(axis).bit_length() - 1)]


def power_of_two(axis):
    return lax.axis_size(axis) & (lax.axis_size(axis) - 1) == 0


def share_flux(value):
    owners, columns, rows = value.shape
    groups = lax.axis_size("lev")
    if not (power_of_two("lev") and power_of_two("wav")):
        copies = jnp.broadcast_to(value[None], (groups,) + value.shape)
        return exchange(copies.reshape(groups * owners, columns, rows))
    for bit in bits_of("lev"):
        value = swap(value, "lev", bit, None)
    bits = bits_of("wav")
    value = value.reshape((2,) * len(bits) + (groups, columns, rows))
    for index, bit in enumerate(bits):
        value = swap(value, "wav", bit, len(bits) - 1 - index)
    value = value.reshape(owners, groups, columns, rows).transpose(1, 0, 2, 3)
    return value.reshape(groups * owners, columns, rows)


def wave_table(waves, valid, unit, lon_count):
    devices, count = waves.shape
    waves = jnp.where(valid, waves, -1).reshape(devices, count // unit, 1, unit)
    waves = jnp.broadcast_to(waves, (devices, count // unit, 2, unit)).reshape(-1, 1)
    rows = waves.shape[0]
    block = math.gcd(rows, 128)
    if block % (2 * unit):
        block = rows
    return pl.pallas_call(
        functools.partial(table_kernel, unit, lon_count),
        grid=(rows // block,),
        in_specs=[pl.BlockSpec((block, 1), lambda i: (i, 0))],
        out_specs=pl.BlockSpec((block, lon_count), lambda i: (i, 0)),
        out_shape=jax.ShapeDtypeStruct((rows, lon_count), jnp.bfloat16),
    )(waves)


def fourier_kernel(
    owners, slots_owner, slots_dev, start, units, waves_ref, rows_ref, fourier_ref, table_ref
):
    rows, lon_count = table_ref.shape
    tile_rows = 4 * UNIT

    @pl.when(pl.program_id(0) == 0)
    def _():
        lane = lax.broadcasted_iota(jnp.int32, (tile_rows, LANES), 1)
        row = lax.broadcasted_iota(jnp.int32, (tile_rows, LANES), 0)
        half = row // UNIT % 2
        first = lane == 0
        scale = math.sqrt(2.0 / lon_count)

        def tile(index, carry):
            waves = jnp.zeros((tile_rows, LANES), jnp.int32)
            for part in range(2):
                group = index * 2 + part
                device = group // units
                slot = (device % owners) * slots_owner + (device // owners) * slots_dev
                slot = slot + start + group % units * UNIT
                for i in range(UNIT):
                    here = (row // (2 * UNIT) == part) & (row % UNIT == i)
                    waves = jnp.where(here, waves_ref[slot + i], waves)
            steps = waves * lane + half * (lon_count // 4)
            steps = jnp.where(first, waves * LANES, steps).astype(jnp.float32)
            steps = steps - lon_count * jnp.round(steps * (1.0 / lon_count))
            angle = steps * (2.0 * math.pi / lon_count)
            cosine, sine = jnp.cos(angle), jnp.sin(angle)
            cos_step = jnp.broadcast_to(cosine[:, :1], cosine.shape)
            sin_step = jnp.broadcast_to(sine[:, :1], sine.shape)
            turn = half.astype(jnp.float32)
            cosine = scale * jnp.where(first, 1.0 - turn, cosine)
            sine = scale * jnp.where(first, turn, sine)
            place = pl.ds(pl.multiple_of(index * tile_rows, tile_rows), tile_rows)
            for column in range(lon_count // LANES):
                table_ref[place, column * LANES : (column + 1) * LANES] = cosine.astype(
                    jnp.bfloat16
                )
                cosine, sine = (
                    cosine * cos_step - sine * sin_step,
                    sine * cos_step + cosine * sin_step,
                )
            return carry

        tiles = rows // tile_rows
        lax.fori_loop(0, tiles, tile, 0, unroll=math.gcd(tiles, 8))

    fourier_ref[...] = lax.dot_general(
        table_ref[...], rows_ref[...], (((1,), (1,)), ((), ())), preferred_element_type=jnp.float32
    ).astype(jnp.bfloat16)


def fourier_call(waves, rows_flat, owners, devices, slots_owner, slots_dev, start, count):
    cells, lon_count = rows_flat.shape
    rows = devices * 2 * count
    block = math.gcd(cells, BLOCK)
    body = functools.partial(
        fourier_kernel, owners, slots_owner, slots_dev, start, count // UNIT
    )
    return pl.pallas_call(
        body,
        grid_spec=pltpu.PrefetchScalarGridSpec(
            num_scalar_prefetch=1,
            grid=(cells // block,),
            in_specs=[pl.BlockSpec((block, lon_count), lambda i, waves: (i, 0))],
            out_specs=[
                pl.BlockSpec((rows, block), lambda i, waves: (0, i)),
                pl.BlockSpec((rows, lon_count), lambda i, waves: (0, 0)),
            ],
        ),
        out_shape=[
            pltpu.HBM((rows, cells), jnp.bfloat16),
            pltpu.HBM((rows, lon_count), jnp.bfloat16),
        ],
        compiler_params=pltpu.CompilerParams(vmem_limit_bytes=32 * 1024 * 1024),
    )(waves, pltpu.with_memory_space_constraint(rows_flat, pltpu.HBM))


def segments(length, source, target):
    cuts = {0}
    cuts.update(i for i in range(1, length) if (source + i) % LANES == 0)
    cuts.update(i for i in range(1, length) if (target + i) % LANES == 0)
    return [
        ((source + i) // LANES, (target + i) // LANES, (target + i) % LANES) for i in sorted(cuts)
    ]


def move_runs(load, store, lane, runs):
    tile, value = 0, None
    for index, source, target, length in runs:
        for src, dst, low in segments(length, source, target):
            piece = pltpu.roll(load(index, src), (target - source) % LANES, 1) if (
                target - source
            ) % LANES else load(index, src)
            if dst != tile:
                store(tile, value)
                tile, value = dst, None
            value = piece if low == 0 else jnp.where(lane >= low, piece, value)
    store(tile, value)


def spectral_kernel(
    groups,
    owners,
    lev_dev,
    lat_dev,
    base_ref,
    waves_ref,
    arrived_ref,
    leg_ref,
    analysis_ref,
    synthesis_ref,
    damping_ref,
    weights_ref,
    sent_ref,
    flux_ref,
    stage_ref,
):
    rows = 2 * UNIT
    levels = groups * lev_dev
    wave_count = leg_ref.shape[2]
    width = owners * lat_dev
    unit = pl.program_id(0)
    lane = lax.broadcasted_iota(jnp.int32, (rows, LANES), 1)

    def take(group, carry):
        for x in range(lev_dev):
            first = pl.multiple_of((group * lev_dev + x) * rows, rows)

            def load(owner, tile):
                part = arrived_ref[group * owners + owner, :, tile * LANES : (tile + 1) * LANES]
                return part.astype(jnp.float32)

            def store(tile, value):
                stage_ref[tile, pl.ds(first, rows), :] = value

            move_runs(
                load,
                store,
                lane,
                [(w, x * lat_dev, w * lat_dev, lat_dev) for w in range(owners)],
            )
        return carry

    lax.fori_loop(0, groups, take, 0)
    degree = lax.broadcasted_iota(jnp.int32, (2 * levels, wave_count), 1)
    flux_row = lax.broadcasted_iota(jnp.int32, (16, wave_count), 0)

    def solve(slot, carry):
        halves = [
            [
                stage_ref[tile, pl.ds(k * UNIT + slot, levels, stride=rows), :]
                for tile in range(width // LANES)
            ]
            for k in range(2)
        ]
        fields = jnp.concatenate([jnp.concatenate(half, axis=1) for half in halves], axis=0)
        leg = leg_ref[slot]
        spectra = jnp.dot(fields.astype(jnp.bfloat16), leg, preferred_element_type=jnp.float32)
        wave = waves_ref[unit * UNIT + slot]
        spectra = jnp.where(degree >= wave, spectra, 0.0).astype(jnp.bfloat16)
        solved, flux = [], 0.0
        for k in range(2):
            modal = jnp.dot(
                analysis_ref[...],
                spectra[k * levels : (k + 1) * levels],
                preferred_element_type=jnp.float32,
            )
            modal = (modal * damping_ref[...]).astype(jnp.bfloat16)
            part = jnp.dot(
                synthesis_ref[...], modal, preferred_element_type=jnp.float32
            ).astype(jnp.bfloat16)
            coef = jnp.sum(weights_ref[...] * part.astype(jnp.float32), axis=0, keepdims=True)
            flux = jnp.where(flux_row == k, coef, flux)
            solved.append(part)
        solved.append(flux.astype(jnp.bfloat16))
        grid = lax.dot_general(
            jnp.concatenate(solved, axis=0),
            leg,
            (((1,), (1,)), ((), ())),
            preferred_element_type=jnp.float32,
        )
        for k in range(2):
            for tile in range(width // LANES):
                stage_ref[tile, pl.ds(k * UNIT + slot, levels, stride=rows), :] = grid[
                    k * levels : (k + 1) * levels, tile * LANES : (tile + 1) * LANES
                ]
            flux_ref[0, pl.ds(k * UNIT + slot, 1), :] = grid[2 * levels + k : 2 * levels + k + 1]
        return carry

    lax.fori_loop(0, UNIT, solve, 0)

    def send(group, carry):
        for w in range(owners):

            def load(x, tile):
                first = pl.multiple_of((group * lev_dev + x) * rows, rows)
                return stage_ref[tile, pl.ds(first, rows), :]

            def store(tile, value):
                sent_ref[group * owners + w, :, tile * LANES : (tile + 1) * LANES] = value.astype(
                    jnp.bfloat16
                )

            move_runs(
                load,
                store,
                lane,
                [(x, w * lat_dev, x * lat_dev, lat_dev) for x in range(lev_dev)],
            )
        return carry

    lax.fori_loop(0, groups, send, 0)


def spectral_call(
    arrived,
    legendre,
    base,
    waves,
    analysis,
    synthesis,
    damping,
    weights,
    groups,
    owners,
    lev_dev,
    lat_dev,
):
    devices, columns, cells = arrived.shape
    units = columns // (2 * UNIT)
    levels = groups * lev_dev
    rows_all, wave_count = legendre.shape[1:]
    body = functools.partial(spectral_kernel, groups, owners, lev_dev, lat_dev)
    whole = lambda shape: pl.BlockSpec(shape, lambda i, base, waves: (0,) * len(shape))
    return pl.pallas_call(
        body,
        grid_spec=pltpu.PrefetchScalarGridSpec(
            num_scalar_prefetch=2,
            grid=(units,),
            in_specs=[
                pl.BlockSpec((devices, 2 * UNIT, cells), lambda i, base, waves: (0, i, 0)),
                pl.BlockSpec(
                    (UNIT, rows_all, wave_count), lambda i, base, waves: (base[0] + i, 0, 0)
                ),
                whole(analysis.shape),
                whole(synthesis.shape),
                whole(damping.shape),
                whole((levels, 1)),
            ],
            out_specs=[
                pl.BlockSpec((devices, 2 * UNIT, cells), lambda i, base, waves: (0, i, 0)),
                pl.BlockSpec((1, 2 * UNIT, rows_all), lambda i, base, waves: (i, 0, 0)),
            ],
            scratch_shapes=[
                pltpu.VMEM((rows_all // LANES, levels * 2 * UNIT, LANES), jnp.float32)
            ],
        ),
        out_shape=[
            pltpu.HBM(arrived.shape, jnp.bfloat16),
            jax.ShapeDtypeStruct((units, 2 * UNIT, rows_all), jnp.float32),
        ],
        compiler_params=pltpu.CompilerParams(vmem_limit_bytes=48 * 1024 * 1024),
    )(base, waves, arrived, legendre, analysis, synthesis, damping, weights.reshape(levels, 1))


def split_slots(count, unit):
    total = sum(CHUNKS) * unit
    if count % total:
        return [(0, count)]
    start, out = 0, []
    for part in CHUNKS:
        part = count // sum(CHUNKS) * part
        out.append((start, part))
        start += part
    return out


def ocean(ocean_temp, diffusivity, surface_heat, land_mask):
    ocean_levels = ocean_temp.shape[0]
    ocean_mask = land_mask.astype(jnp.float32)
    level_one = (jnp.arange(ocean_levels, dtype=jnp.int32) == 0).astype(jnp.float32)[:, None, None]
    ocean_now = ocean_temp * ocean_mask[None]
    stacked = jnp.concatenate(
        [ocean_now, ocean_mask[None], diffusivity[None], surface_heat[None]], axis=0
    )
    padded = with_halo(stacked.astype(jnp.bfloat16), (("lev", 1), ("wav", 2)), SWEEPS).astype(
        stacked.dtype
    )
    current = padded[:ocean_levels]
    for sweep_idx in range(SWEEPS):
        margin = sweep_idx + 1
        inside = current[:, 1:-1, 1:-1]
        laplace = (
            current[:, 2:, 1:-1]
            + current[:, :-2, 1:-1]
            + current[:, 1:-1, 2:]
            + current[:, 1:-1, :-2]
            - 4.0 * inside
        )
        mask_in = padded[ocean_levels, margin:-margin, margin:-margin]
        kappa_in = padded[ocean_levels + 1, margin:-margin, margin:-margin]
        heat_in = padded[ocean_levels + 2, margin:-margin, margin:-margin]
        current = mask_in[None] * (inside + kappa_in[None] * laplace + level_one * heat_in[None])
    return current


def per_device(
    grid_field,
    legendre,
    wave_of_slot,
    lat_of_row,
    analysis,
    synthesis,
    mode_rates,
    flux_weights,
    remap_mats,
    pair_dest,
    pair_src,
    pair_dst,
    ocean_temp,
    diffusivity,
    surface_heat,
    land_mask,
):
    groups = lax.axis_size("lev")
    owners = lax.axis_size("wav")
    devices = groups * owners
    my_group = lax.axis_index("lev")
    my_owner = lax.axis_index("wav")
    lev_dev, lat_dev, lon_count = grid_field.shape
    wave_count = wave_of_slot.shape[0]
    slots_owner = wave_count // owners
    slots_dev = -(-slots_owner // groups)
    cells = lev_dev * lat_dev
    rows_flat = grid_field.reshape(cells, lon_count)
    degree = jnp.arange(wave_count, dtype=jnp.int32)
    damp_base = (degree * (degree + 1)).astype(jnp.float32) / float(wave_count * wave_count)
    damping = 1.0 / (1.0 + mode_rates[:, None] * damp_base[None, :])

    def slots_of(group, owner, start, count):
        local = group * slots_dev + start + jnp.arange(count, dtype=jnp.int32)
        slot = owner * slots_owner + jnp.minimum(local, slots_owner - 1)
        return local, wave_of_slot[slot], local < slots_owner

    exact = slots_owner == slots_dev * groups
    fused = (
        exact
        and slots_dev % UNIT == 0
        and lon_count % LANES == 0
        and cells % LANES == 0
        and owners * lat_dev % LANES == 0
        and groups * lev_dev % 8 == 0
    )
    unit = UNIT if fused else slots_dev
    chunks = split_slots(slots_dev, unit)
    spare = groups * slots_dev - slots_owner
    all_waves = jnp.pad(wave_of_slot.reshape(owners, slots_owner), ((0, 0), (0, spare)))
    all_waves = all_waves.reshape(owners, groups, slots_dev).transpose(1, 0, 2)
    all_valid = jnp.arange(groups * slots_dev, dtype=jnp.int32) < slots_owner
    all_valid = jnp.broadcast_to(all_valid.reshape(groups, 1, slots_dev), all_waves.shape)
    all_waves = all_waves.reshape(devices, slots_dev)
    all_valid = all_valid.reshape(devices, slots_dev)

    def forward(start, count):
        if fused:
            fourier, table = fourier_call(
                wave_of_slot, rows_flat, owners, devices, slots_owner, slots_dev, start, count
            )
            return table, fourier.reshape(devices, 2 * count, cells)
        chosen = slice(start, start + count)
        table = wave_table(all_waves[:, chosen], all_valid[:, chosen], unit, lon_count)
        fourier = lax.dot_general(
            table, rows_flat, (((1,), (1,)), ((), ())), preferred_element_type=jnp.float32
        ).astype(jnp.bfloat16)
        return table, fourier.reshape(devices, 2 * count, cells)

    def spectral_fused(arrived, start, count):
        base = my_group * (slots_dev // UNIT) + start // UNIT
        first = my_owner * slots_owner + my_group * slots_dev + start
        my_waves = lax.dynamic_slice_in_dim(wave_of_slot, first, count)
        grid_coef, flux_lat = spectral_call(
            arrived,
            legendre,
            base.astype(jnp.int32).reshape(1),
            my_waves,
            analysis,
            synthesis,
            damping,
            flux_weights,
            groups,
            owners,
            lev_dev,
            lat_dev,
        )
        return grid_coef, flux_lat.astype(jnp.bfloat16).reshape(2 * count, owners, lat_dev)

    def spectral(arrived, start, count):
        arrived, my_analysis, my_synthesis, my_damping, my_weights = lax.optimization_barrier(
            (arrived, analysis, synthesis, damping, flux_weights)
        )
        local, my_waves, _ = slots_of(my_group, my_owner, start, count)
        if exact:
            leg = lax.dynamic_slice_in_dim(legendre, my_group * slots_dev + start, count, axis=0)
        else:
            leg = jnp.take(legendre, jnp.minimum(local, slots_owner - 1), axis=0)
        fields = arrived.reshape(groups, owners, 2, count, lev_dev, lat_dev)
        fields = fields.transpose(3, 1, 2, 0, 4, 5).reshape(
            count, owners, 2 * groups * lev_dev, lat_dev
        )
        leg_rows = leg.reshape(count, owners, lat_dev, wave_count)
        spectra = jnp.einsum(
            "swmr,swrn->smn", fields, leg_rows, preferred_element_type=jnp.float32
        ).reshape(count, 2, groups * lev_dev, wave_count)
        retained = degree[None, :] >= my_waves[:, None]
        spectra = jnp.where(retained[:, None, None, :], spectra, 0.0).astype(jnp.bfloat16)
        modal_coef = jnp.einsum(
            "ix,skxn->skin", my_analysis, spectra, preferred_element_type=jnp.float32
        )
        modal_coef = (modal_coef * my_damping[None, None]).astype(jnp.bfloat16)
        solved = jnp.einsum(
            "xi,skin->skxn", my_synthesis, modal_coef, preferred_element_type=jnp.float32
        ).astype(jnp.bfloat16)
        flux_coef = jnp.sum(
            my_weights[None, None, :, None] * solved.astype(jnp.float32), axis=2
        ).astype(jnp.bfloat16)
        grid_coef = jnp.einsum(
            "smn,swrn->swmr",
            solved.reshape(count, 2 * groups * lev_dev, wave_count),
            leg_rows,
            preferred_element_type=jnp.float32,
        ).astype(jnp.bfloat16)
        grid_coef = grid_coef.reshape(count, owners, 2, groups, lev_dev, lat_dev)
        grid_coef = grid_coef.transpose(3, 1, 2, 0, 4, 5).reshape(devices, 2 * count, cells)
        flux_lat = lax.dot_general(
            flux_coef, leg, (((2,), (2,)), ((0,), (0,))), preferred_element_type=jnp.float32
        ).astype(jnp.bfloat16)
        flux_lat = flux_lat.reshape(count, 2, owners, lat_dev).transpose(1, 0, 2, 3)
        return grid_coef, flux_lat.reshape(2 * count, owners, lat_dev)

    tables, arrivals, returned, sent, flux_parts = [], [], [], [], []
    for chunk in chunks:
        table, fourier = forward(*chunk)
        tables.append(table)
        arrivals.append(exchange(fourier))
    for index, chunk in enumerate(chunks):
        step = spectral_fused if fused else spectral
        grid_coef, flux_lat = step(arrivals[index], *chunk)
        sent.append(grid_coef)
        flux_parts.append(flux_lat)
    for value in sent:
        returned.append(exchange(value))
    flux_lat = jnp.concatenate(flux_parts, axis=0).transpose(1, 0, 2)
    flux_back = share_flux(flux_lat)

    flux_grid = 0.0
    for (start, count), table in zip(chunks, tables):
        part = flux_back[:, 2 * start : 2 * (start + count)].reshape(-1, lat_dev)
        flux_grid += lax.dot_general(
            part, table, (((0,), (0,)), ((), ())), preferred_element_type=jnp.float32
        )
    flux_grid = flux_grid.astype(jnp.bfloat16)

    latitude = jnp.sin(
        math.pi * (lat_of_row.astype(jnp.float32) + 0.5) / (lat_dev * owners) - math.pi / 2
    )
    latitude = jnp.broadcast_to(latitude[None], (lev_dev, lat_dev)).reshape(cells, 1)
    regridded = 0.0
    for index in range(len(chunks)):
        regridded += lax.dot_general(
            returned[index].reshape(-1, cells),
            tables[index],
            (((0,), (0,)), ((), ())),
            preferred_element_type=jnp.float32,
        )
        if index + 1 < len(chunks):
            regridded = lax.optimization_barrier(regridded.astype(jnp.bfloat16))
            regridded = regridded.astype(jnp.float32)
    atm_out = regridded * (1.0 + rows_flat.astype(jnp.float32) * latitude)
    atm_out = atm_out.astype(jnp.bfloat16).reshape(lev_dev, lat_dev, lon_count)

    ocean_now = ocean(ocean_temp, diffusivity, surface_heat, land_mask)

    ocean_rows, ocean_cols = diffusivity.shape
    pieces = lon_count // ocean_cols
    segments = flux_grid.reshape(lat_dev * pieces, ocean_cols)
    pairs_dev = remap_mats.shape[1]
    all_dest = pair_dest[0, :, 0].reshape(owners, pairs_dev)
    all_dst = pair_dst[0].reshape(owners, pairs_dev)
    earlier = jnp.arange(pairs_dev)[None, :] < jnp.arange(pairs_dev)[:, None]
    rank = jnp.sum(
        (all_dest[:, :, None] == all_dest[:, None, :]) & earlier[None], axis=2, dtype=jnp.int32
    )
    my_src = lax.dynamic_slice_in_dim(pair_src[0], my_owner * pairs_dev, pairs_dev)
    chosen = jnp.take(segments, my_src, axis=0)
    products = jnp.einsum("pij,pj->pi", remap_mats[0], chosen, preferred_element_type=jnp.float32)
    place = lax.dynamic_index_in_dim(all_dest * CAP + rank, my_owner, 0, keepdims=False)
    outgoing = jnp.dot(
        (jnp.arange(owners * CAP, dtype=jnp.int32)[:, None] == place[None, :]).astype(jnp.float32),
        products,
        precision=lax.Precision.HIGHEST,
        preferred_element_type=jnp.float32,
    )
    outgoing = outgoing.reshape(owners, CAP, ocean_cols)
    incoming = lax.all_to_all(outgoing, "wav", split_axis=0, concat_axis=0, tiled=True)
    mine = (all_dest == my_owner)[:, None, :] & (
        rank[:, None, :] == jnp.arange(CAP, dtype=jnp.int32)[None, :, None]
    )
    row_hit = all_dst[None, :, None, :] == jnp.arange(ocean_rows, dtype=jnp.int32)[:, None, None, None]
    picker = jnp.any(mine[None] & row_hit, axis=3).astype(jnp.float32)
    ocean_flux = jnp.dot(
        picker.reshape(ocean_rows, owners * CAP),
        incoming.reshape(owners * CAP, ocean_cols),
        precision=lax.Precision.HIGHEST,
        preferred_element_type=jnp.float32,
    )
    return (atm_out, ocean_now, ocean_flux)


def solution(mesh):
    return jax.shard_map(
        per_device,
        mesh=mesh,
        in_specs=(
            P("lev", "wav", None),
            P("wav", None, None),
            P(),
            P("wav"),
            P(),
            P(),
            P(),
            P(),
            P("lev", "wav", None, None),
            P("lev", None, None),
            P("lev", None),
            P("lev", None),
            P(None, "lev", "wav"),
            P("lev", "wav"),
            P("lev", "wav"),
            P("lev", "wav"),
        ),
        out_specs=(P("lev", "wav", None), P(None, "lev", "wav"), P("lev", "wav")),
        check_vma=False,
    )
```

```python
import functools
import math

import jax
import jax.numpy as jnp
from jax import lax
from jax.experimental import pallas as pl
from jax.experimental.pallas import tpu as pltpu
from jax.sharding import PartitionSpec as P


SWEEPS = 4
CAP = 2
AXES = ("lev", "wav")
CHUNKS = (3, 2)
UNIT = 4
BLOCK = 1280
LANES = 128


def with_halo(value, sides, width):
    for axis, dim in sides:
        count, length = (lax.axis_size(axis), value.shape[dim])
        up = [(i, (i + 1) % count) for i in range(count - 1)]
        down = [(j, i) for i, j in up]
        last = lax.slice_in_dim(value, length - width, length, axis=dim)
        initial = lax.slice_in_dim(value, 0, width, axis=dim)
        before = lax.ppermute(last, axis, up)
        after = lax.ppermute(initial, axis, down)
        value = jnp.concatenate([before, value, after], axis=dim)
    return value


def exchange(value):
    return lax.all_to_all(value, AXES, split_axis=0, concat_axis=0, tiled=True)


def table_kernel(unit, lon_count, waves_ref, table_ref):
    rows = waves_ref.shape[0]
    lane = lax.broadcasted_iota(jnp.int32, (rows, LANES), 1)
    half = (lax.broadcasted_iota(jnp.int32, (rows, LANES), 0) // unit) % 2
    waves = jnp.broadcast_to(waves_ref[...], (rows, LANES))
    scale = jnp.where(waves < 0, 0.0, math.sqrt(2.0 / lon_count))

    def angle(steps):
        steps = steps.astype(jnp.float32)
        steps = steps - lon_count * jnp.round(steps * (1.0 / lon_count))
        return steps * (2.0 * math.pi / lon_count)

    low = angle(waves * lane + half * (lon_count // 4))
    high = angle(waves * (lane * LANES))
    cos_low, sin_low = scale * jnp.cos(low), scale * jnp.sin(low)
    cos_high, sin_high = jnp.cos(high), jnp.sin(high)
    for tile in range(lon_count // LANES):
        part = cos_low * cos_high[:, tile : tile + 1] - sin_low * sin_high[:, tile : tile + 1]
        table_ref[:, tile * LANES : (tile + 1) * LANES] = part.astype(jnp.bfloat16)


def swap(value, axis, bit, place):
    pairs = [(i, i ^ bit) for i in range(lax.axis_size(axis))]
    mine = (lax.axis_index(axis) // bit) % 2
    if place is None:
        kept = sent = value
        place = 1
    else:
        kept = lax.dynamic_index_in_dim(value, mine, place, keepdims=False)
        sent = lax.dynamic_index_in_dim(value, 1 - mine, place, keepdims=False)
    came = lax.ppermute(sent, axis, pairs)
    first = jnp.where(mine == 0, kept, came)
    second = jnp.where(mine == 0, came, kept)
    return jnp.stack([first, second], axis=place)


def bits_of(axis):
    return [1 << i for i in range(lax.axis_size(axis).bit_length() - 1)]


def power_of_two(axis):
    return lax.axis_size(axis) & (lax.axis_size(axis) - 1) == 0


def share_flux(value):
    owners, columns, rows = value.shape
    groups = lax.axis_size("lev")
    if not (power_of_two("lev") and power_of_two("wav")):
        copies = jnp.broadcast_to(value[None], (groups,) + value.shape)
        return exchange(copies.reshape(groups * owners, columns, rows))
    for bit in bits_of("lev"):
        value = swap(value, "lev", bit, None)
    bits = bits_of("wav")
    value = value.reshape((2,) * len(bits) + (groups, columns, rows))
    for index, bit in enumerate(bits):
        value = swap(value, "wav", bit, len(bits) - 1 - index)
    value = value.reshape(owners, groups, columns, rows).transpose(1, 0, 2, 3)
    return value.reshape(groups * owners, columns, rows)


def share_pairs(value):
    if not power_of_two("wav"):
        return lax.all_to_all(value, "wav", split_axis=0, concat_axis=0, tiled=True)
    bits = bits_of("wav")
    shape = value.shape
    value = value.reshape((2,) * len(bits) + shape[1:])
    for index, bit in enumerate(bits):
        value = swap(value, "wav", bit, len(bits) - 1 - index)
    return value.reshape(shape)


def wave_table(waves, valid, unit, lon_count):
    devices, count = waves.shape
    waves = jnp.where(valid, waves, -1).reshape(devices, count // unit, 1, unit)
    waves = jnp.broadcast_to(waves, (devices, count // unit, 2, unit)).reshape(-1, 1)
    rows = waves.shape[0]
    block = math.gcd(rows, 128)
    if block % (2 * unit):
        block = rows
    return pl.pallas_call(
        functools.partial(table_kernel, unit, lon_count),
        grid=(rows // block,),
        in_specs=[pl.BlockSpec((block, 1), lambda i: (i, 0))],
        out_specs=pl.BlockSpec((block, lon_count), lambda i: (i, 0)),
        out_shape=jax.ShapeDtypeStruct((rows, lon_count), jnp.bfloat16),
    )(waves)


def fourier_kernel(
    owners, slots_owner, slots_dev, start, units, waves_ref, rows_ref, fourier_ref, table_ref
):
    rows, lon_count = table_ref.shape
    tile_rows = 4 * UNIT

    @pl.when(pl.program_id(0) == 0)
    def _():
        lane = lax.broadcasted_iota(jnp.int32, (tile_rows, LANES), 1)
        row = lax.broadcasted_iota(jnp.int32, (tile_rows, LANES), 0)
        half = row // UNIT % 2
        first = lane == 0
        scale = math.sqrt(2.0 / lon_count)

        def tile(index, carry):
            waves = jnp.zeros((tile_rows, LANES), jnp.int32)
            for part in range(2):
                group = index * 2 + part
                device = group // units
                slot = (device % owners) * slots_owner + (device // owners) * slots_dev
                slot = slot + start + group % units * UNIT
                for i in range(UNIT):
                    here = (row // (2 * UNIT) == part) & (row % UNIT == i)
                    waves = jnp.where(here, waves_ref[slot + i], waves)
            steps = waves * lane + half * (lon_count // 4)
            steps = jnp.where(first, waves * LANES, steps).astype(jnp.float32)
            steps = steps - lon_count * jnp.round(steps * (1.0 / lon_count))
            angle = steps * (2.0 * math.pi / lon_count)
            cosine, sine = jnp.cos(angle), jnp.sin(angle)
            cos_step = jnp.broadcast_to(cosine[:, :1], cosine.shape)
            sin_step = jnp.broadcast_to(sine[:, :1], sine.shape)
            turn = half.astype(jnp.float32)
            cosine = scale * jnp.where(first, 1.0 - turn, cosine)
            sine = scale * jnp.where(first, turn, sine)
            place = pl.ds(pl.multiple_of(index * tile_rows, tile_rows), tile_rows)
            for column in range(lon_count // LANES):
                table_ref[place, column * LANES : (column + 1) * LANES] = cosine.astype(
                    jnp.bfloat16
                )
                cosine, sine = (
                    cosine * cos_step - sine * sin_step,
                    sine * cos_step + cosine * sin_step,
                )
            return carry

        tiles = rows // tile_rows
        lax.fori_loop(0, tiles, tile, 0, unroll=math.gcd(tiles, 8))

    fourier_ref[...] = lax.dot_general(
        table_ref[...], rows_ref[...], (((1,), (1,)), ((), ())), preferred_element_type=jnp.float32
    ).astype(jnp.bfloat16)


def fourier_call(waves, rows_flat, owners, devices, slots_owner, slots_dev, start, count):
    cells, lon_count = rows_flat.shape
    rows = devices * 2 * count
    block = math.gcd(cells, BLOCK)
    body = functools.partial(
        fourier_kernel, owners, slots_owner, slots_dev, start, count // UNIT
    )
    return pl.pallas_call(
        body,
        grid_spec=pltpu.PrefetchScalarGridSpec(
            num_scalar_prefetch=1,
            grid=(cells // block,),
            in_specs=[pl.BlockSpec((block, lon_count), lambda i, waves: (i, 0))],
            out_specs=[
                pl.BlockSpec((rows, block), lambda i, waves: (0, i)),
                pl.BlockSpec((rows, lon_count), lambda i, waves: (0, 0)),
            ],
        ),
        out_shape=[
            pltpu.HBM((rows, cells), jnp.bfloat16),
            pltpu.HBM((rows, lon_count), jnp.bfloat16),
        ],
        compiler_params=pltpu.CompilerParams(vmem_limit_bytes=32 * 1024 * 1024),
    )(waves, pltpu.with_memory_space_constraint(rows_flat, pltpu.HBM))


def final_kernel(lat_dev, returned_ref, table_ref, partial_ref, rows_ref, latitude_ref, out_ref):
    total = partial_ref[...].astype(jnp.float32) + lax.dot_general(
        returned_ref[...],
        table_ref[...],
        (((0,), (0,)), ((), ())),
        preferred_element_type=jnp.float32,
    )
    shape = (out_ref.shape[0] // lat_dev, lat_dev, out_ref.shape[1])
    field = rows_ref[...].astype(jnp.float32).reshape(shape)
    total = total.reshape(shape) * (1.0 + field * latitude_ref[...][None])
    out_ref[...] = total.reshape(out_ref.shape).astype(jnp.bfloat16)


def final_call(returned, table, partial, rows_flat, latitude):
    cells, lon_count = rows_flat.shape
    lat_dev = latitude.shape[0]
    columns = returned.shape[0]
    block = lat_dev * 16
    rows = pl.BlockSpec((block, lon_count), lambda i: (i, 0))
    return pl.pallas_call(
        functools.partial(final_kernel, lat_dev),
        grid=(cells // block,),
        in_specs=[
            pl.BlockSpec((columns, block), lambda i: (0, i)),
            pl.BlockSpec((columns, lon_count), lambda i: (0, 0)),
            rows,
            rows,
            pl.BlockSpec((lat_dev, 1), lambda i: (0, 0)),
        ],
        out_specs=rows,
        out_shape=pltpu.HBM((cells, lon_count), jnp.bfloat16),
        compiler_params=pltpu.CompilerParams(vmem_limit_bytes=32 * 1024 * 1024),
    )(
        pltpu.with_memory_space_constraint(returned, pltpu.HBM),
        table,
        pltpu.with_memory_space_constraint(partial, pltpu.HBM),
        pltpu.with_memory_space_constraint(rows_flat, pltpu.HBM),
        latitude[:, None],
    )


def segments(length, source, target):
    cuts = {0}
    cuts.update(i for i in range(1, length) if (source + i) % LANES == 0)
    cuts.update(i for i in range(1, length) if (target + i) % LANES == 0)
    return [
        ((source + i) // LANES, (target + i) // LANES, (target + i) % LANES) for i in sorted(cuts)
    ]


def move_runs(load, store, lane, runs):
    tile, value = 0, None
    for index, source, target, length in runs:
        for src, dst, low in segments(length, source, target):
            piece = pltpu.roll(load(index, src), (target - source) % LANES, 1) if (
                target - source
            ) % LANES else load(index, src)
            if dst != tile:
                store(tile, value)
                tile, value = dst, None
            value = piece if low == 0 else jnp.where(lane >= low, piece, value)
    store(tile, value)


def spectral_kernel(
    groups,
    owners,
    lev_dev,
    lat_dev,
    base_ref,
    waves_ref,
    arrived_ref,
    leg_ref,
    analysis_ref,
    synthesis_ref,
    damping_ref,
    weights_ref,
    sent_ref,
    flux_ref,
    stage_ref,
):
    rows = 2 * UNIT
    levels = groups * lev_dev
    wave_count = leg_ref.shape[2]
    width = owners * lat_dev
    unit = pl.program_id(0)
    lane = lax.broadcasted_iota(jnp.int32, (rows, LANES), 1)

    def take(group, carry):
        for x in range(lev_dev):
            first = pl.multiple_of((group * lev_dev + x) * rows, rows)

            def load(owner, tile):
                part = arrived_ref[group * owners + owner, :, tile * LANES : (tile + 1) * LANES]
                return part.astype(jnp.float32)

            def store(tile, value):
                stage_ref[tile, pl.ds(first, rows), :] = value

            move_runs(
                load,
                store,
                lane,
                [(w, x * lat_dev, w * lat_dev, lat_dev) for w in range(owners)],
            )
        return carry

    lax.fori_loop(0, groups, take, 0)
    degree = lax.broadcasted_iota(jnp.int32, (2 * levels, wave_count), 1)
    flux_row = lax.broadcasted_iota(jnp.int32, (16, wave_count), 0)

    def solve(slot, carry):
        halves = [
            [
                stage_ref[tile, pl.ds(k * UNIT + slot, levels, stride=rows), :]
                for tile in range(width // LANES)
            ]
            for k in range(2)
        ]
        fields = jnp.concatenate([jnp.concatenate(half, axis=1) for half in halves], axis=0)
        leg = leg_ref[slot]
        spectra = jnp.dot(fields.astype(jnp.bfloat16), leg, preferred_element_type=jnp.float32)
        wave = waves_ref[unit * UNIT + slot]
        spectra = jnp.where(degree >= wave, spectra, 0.0).astype(jnp.bfloat16)
        solved, flux = [], 0.0
        for k in range(2):
            modal = jnp.dot(
                analysis_ref[...],
                spectra[k * levels : (k + 1) * levels],
                preferred_element_type=jnp.float32,
            )
            modal = (modal * damping_ref[...]).astype(jnp.bfloat16)
            part = jnp.dot(
                synthesis_ref[...], modal, preferred_element_type=jnp.float32
            ).astype(jnp.bfloat16)
            coef = jnp.sum(weights_ref[...] * part.astype(jnp.float32), axis=0, keepdims=True)
            flux = jnp.where(flux_row == k, coef, flux)
            solved.append(part)
        solved.append(flux.astype(jnp.bfloat16))
        grid = lax.dot_general(
            jnp.concatenate(solved, axis=0),
            leg,
            (((1,), (1,)), ((), ())),
            preferred_element_type=jnp.float32,
        )
        for k in range(2):
            for tile in range(width // LANES):
                stage_ref[tile, pl.ds(k * UNIT + slot, levels, stride=rows), :] = grid[
                    k * levels : (k + 1) * levels, tile * LANES : (tile + 1) * LANES
                ]
            flux_ref[0, pl.ds(k * UNIT + slot, 1), :] = grid[2 * levels + k : 2 * levels + k + 1]
        return carry

    lax.fori_loop(0, UNIT, solve, 0)

    def send(group, carry):
        for w in range(owners):

            def load(x, tile):
                first = pl.multiple_of((group * lev_dev + x) * rows, rows)
                return stage_ref[tile, pl.ds(first, rows), :]

            def store(tile, value):
                sent_ref[group * owners + w, :, tile * LANES : (tile + 1) * LANES] = value.astype(
                    jnp.bfloat16
                )

            move_runs(
                load,
                store,
                lane,
                [(x, w * lat_dev, x * lat_dev, lat_dev) for x in range(lev_dev)],
            )
        return carry

    lax.fori_loop(0, groups, send, 0)


def spectral_call(
    arrived,
    legendre,
    base,
    waves,
    analysis,
    synthesis,
    damping,
    weights,
    groups,
    owners,
    lev_dev,
    lat_dev,
):
    devices, columns, cells = arrived.shape
    units = columns // (2 * UNIT)
    levels = groups * lev_dev
    rows_all, wave_count = legendre.shape[1:]
    body = functools.partial(spectral_kernel, groups, owners, lev_dev, lat_dev)
    whole = lambda shape: pl.BlockSpec(shape, lambda i, base, waves: (0,) * len(shape))
    return pl.pallas_call(
        body,
        grid_spec=pltpu.PrefetchScalarGridSpec(
            num_scalar_prefetch=2,
            grid=(units,),
            in_specs=[
                pl.BlockSpec((devices, 2 * UNIT, cells), lambda i, base, waves: (0, i, 0)),
                pl.BlockSpec(
                    (UNIT, rows_all, wave_count), lambda i, base, waves: (base[0] + i, 0, 0)
                ),
                whole(analysis.shape),
                whole(synthesis.shape),
                whole(damping.shape),
                whole((levels, 1)),
            ],
            out_specs=[
                pl.BlockSpec((devices, 2 * UNIT, cells), lambda i, base, waves: (0, i, 0)),
                pl.BlockSpec((1, 2 * UNIT, rows_all), lambda i, base, waves: (i, 0, 0)),
            ],
            scratch_shapes=[
                pltpu.VMEM((rows_all // LANES, levels * 2 * UNIT, LANES), jnp.float32)
            ],
        ),
        out_shape=[
            pltpu.HBM(arrived.shape, jnp.bfloat16),
            jax.ShapeDtypeStruct((units, 2 * UNIT, rows_all), jnp.float32),
        ],
        compiler_params=pltpu.CompilerParams(vmem_limit_bytes=48 * 1024 * 1024),
    )(base, waves, arrived, legendre, analysis, synthesis, damping, weights.reshape(levels, 1))


def split_slots(count, unit):
    total = sum(CHUNKS) * unit
    if count % total:
        return [(0, count)]
    start, out = 0, []
    for part in CHUNKS:
        part = count // sum(CHUNKS) * part
        out.append((start, part))
        start += part
    return out


def ocean(ocean_temp, diffusivity, surface_heat, land_mask):
    ocean_levels = ocean_temp.shape[0]
    ocean_mask = land_mask.astype(jnp.float32)
    level_one = (jnp.arange(ocean_levels, dtype=jnp.int32) == 0).astype(jnp.float32)[:, None, None]
    ocean_now = ocean_temp * ocean_mask[None]
    stacked = jnp.concatenate(
        [ocean_now, ocean_mask[None], diffusivity[None], surface_heat[None]], axis=0
    )
    padded = with_halo(stacked.astype(jnp.bfloat16), (("lev", 1), ("wav", 2)), SWEEPS).astype(
        stacked.dtype
    )
    current = padded[:ocean_levels]
    for sweep_idx in range(SWEEPS):
        margin = sweep_idx + 1
        inside = current[:, 1:-1, 1:-1]
        laplace = (
            current[:, 2:, 1:-1]
            + current[:, :-2, 1:-1]
            + current[:, 1:-1, 2:]
            + current[:, 1:-1, :-2]
            - 4.0 * inside
        )
        mask_in = padded[ocean_levels, margin:-margin, margin:-margin]
        kappa_in = padded[ocean_levels + 1, margin:-margin, margin:-margin]
        heat_in = padded[ocean_levels + 2, margin:-margin, margin:-margin]
        current = mask_in[None] * (inside + kappa_in[None] * laplace + level_one * heat_in[None])
    return current


def per_device(
    grid_field,
    legendre,
    wave_of_slot,
    lat_of_row,
    analysis,
    synthesis,
    mode_rates,
    flux_weights,
    remap_mats,
    pair_dest,
    pair_src,
    pair_dst,
    ocean_temp,
    diffusivity,
    surface_heat,
    land_mask,
):
    groups = lax.axis_size("lev")
    owners = lax.axis_size("wav")
    devices = groups * owners
    my_group = lax.axis_index("lev")
    my_owner = lax.axis_index("wav")
    lev_dev, lat_dev, lon_count = grid_field.shape
    wave_count = wave_of_slot.shape[0]
    slots_owner = wave_count // owners
    slots_dev = -(-slots_owner // groups)
    cells = lev_dev * lat_dev
    rows_flat = grid_field.reshape(cells, lon_count)
    degree = jnp.arange(wave_count, dtype=jnp.int32)
    damp_base = (degree * (degree + 1)).astype(jnp.float32) / float(wave_count * wave_count)
    damping = 1.0 / (1.0 + mode_rates[:, None] * damp_base[None, :])

    def slots_of(group, owner, start, count):
        local = group * slots_dev + start + jnp.arange(count, dtype=jnp.int32)
        slot = owner * slots_owner + jnp.minimum(local, slots_owner - 1)
        return local, wave_of_slot[slot], local < slots_owner

    exact = slots_owner == slots_dev * groups
    fused = (
        exact
        and slots_dev % UNIT == 0
        and lon_count % LANES == 0
        and cells % LANES == 0
        and owners * lat_dev % LANES == 0
        and groups * lev_dev % 8 == 0
        and lev_dev % 16 == 0
        and lat_dev % 16 == 0
    )
    unit = UNIT if fused else slots_dev
    chunks = split_slots(slots_dev, unit)
    spare = groups * slots_dev - slots_owner
    all_waves = jnp.pad(wave_of_slot.reshape(owners, slots_owner), ((0, 0), (0, spare)))
    all_waves = all_waves.reshape(owners, groups, slots_dev).transpose(1, 0, 2)
    all_valid = jnp.arange(groups * slots_dev, dtype=jnp.int32) < slots_owner
    all_valid = jnp.broadcast_to(all_valid.reshape(groups, 1, slots_dev), all_waves.shape)
    all_waves = all_waves.reshape(devices, slots_dev)
    all_valid = all_valid.reshape(devices, slots_dev)

    def forward(start, count):
        if fused:
            fourier, table = fourier_call(
                wave_of_slot, rows_flat, owners, devices, slots_owner, slots_dev, start, count
            )
            return table, fourier.reshape(devices, 2 * count, cells)
        chosen = slice(start, start + count)
        table = wave_table(all_waves[:, chosen], all_valid[:, chosen], unit, lon_count)
        fourier = lax.dot_general(
            table, rows_flat, (((1,), (1,)), ((), ())), preferred_element_type=jnp.float32
        ).astype(jnp.bfloat16)
        return table, fourier.reshape(devices, 2 * count, cells)

    def spectral_fused(arrived, start, count):
        base = my_group * (slots_dev // UNIT) + start // UNIT
        first = my_owner * slots_owner + my_group * slots_dev + start
        my_waves = lax.dynamic_slice_in_dim(wave_of_slot, first, count)
        grid_coef, flux_lat = spectral_call(
            arrived,
            legendre,
            base.astype(jnp.int32).reshape(1),
            my_waves,
            analysis,
            synthesis,
            damping,
            flux_weights,
            groups,
            owners,
            lev_dev,
            lat_dev,
        )
        return grid_coef, flux_lat.astype(jnp.bfloat16).reshape(2 * count, owners, lat_dev)

    def spectral(arrived, start, count):
        arrived, my_analysis, my_synthesis, my_damping, my_weights = lax.optimization_barrier(
            (arrived, analysis, synthesis, damping, flux_weights)
        )
        local, my_waves, _ = slots_of(my_group, my_owner, start, count)
        if exact:
            leg = lax.dynamic_slice_in_dim(legendre, my_group * slots_dev + start, count, axis=0)
        else:
            leg = jnp.take(legendre, jnp.minimum(local, slots_owner - 1), axis=0)
        fields = arrived.reshape(groups, owners, 2, count, lev_dev, lat_dev)
        fields = fields.transpose(3, 1, 2, 0, 4, 5).reshape(
            count, owners, 2 * groups * lev_dev, lat_dev
        )
        leg_rows = leg.reshape(count, owners, lat_dev, wave_count)
        spectra = jnp.einsum(
            "swmr,swrn->smn", fields, leg_rows, preferred_element_type=jnp.float32
        ).reshape(count, 2, groups * lev_dev, wave_count)
        retained = degree[None, :] >= my_waves[:, None]
        spectra = jnp.where(retained[:, None, None, :], spectra, 0.0).astype(jnp.bfloat16)
        modal_coef = jnp.einsum(
            "ix,skxn->skin", my_analysis, spectra, preferred_element_type=jnp.float32
        )
        modal_coef = (modal_coef * my_damping[None, None]).astype(jnp.bfloat16)
        solved = jnp.einsum(
            "xi,skin->skxn", my_synthesis, modal_coef, preferred_element_type=jnp.float32
        ).astype(jnp.bfloat16)
        flux_coef = jnp.sum(
            my_weights[None, None, :, None] * solved.astype(jnp.float32), axis=2
        ).astype(jnp.bfloat16)
        grid_coef = jnp.einsum(
            "smn,swrn->swmr",
            solved.reshape(count, 2 * groups * lev_dev, wave_count),
            leg_rows,
            preferred_element_type=jnp.float32,
        ).astype(jnp.bfloat16)
        grid_coef = grid_coef.reshape(count, owners, 2, groups, lev_dev, lat_dev)
        grid_coef = grid_coef.transpose(3, 1, 2, 0, 4, 5).reshape(devices, 2 * count, cells)
        flux_lat = lax.dot_general(
            flux_coef, leg, (((2,), (2,)), ((0,), (0,))), preferred_element_type=jnp.float32
        ).astype(jnp.bfloat16)
        flux_lat = flux_lat.reshape(count, 2, owners, lat_dev).transpose(1, 0, 2, 3)
        return grid_coef, flux_lat.reshape(2 * count, owners, lat_dev)

    tables, arrivals, returned, sent, flux_parts = [], [], [], [], []
    for chunk in chunks:
        table, fourier = forward(*chunk)
        tables.append(table)
        arrivals.append(exchange(fourier))
    for index, chunk in enumerate(chunks):
        step = spectral_fused if fused else spectral
        grid_coef, flux_lat = step(arrivals[index], *chunk)
        sent.append(grid_coef)
        flux_parts.append(flux_lat)
    for value in sent:
        returned.append(exchange(value))
    flux_lat = jnp.concatenate(flux_parts, axis=0).transpose(1, 0, 2)
    flux_back = share_flux(flux_lat)

    flux_grid = 0.0
    for (start, count), table in zip(chunks, tables):
        part = flux_back[:, 2 * start : 2 * (start + count)].reshape(-1, lat_dev)
        flux_grid += lax.dot_general(
            part, table, (((0,), (0,)), ((), ())), preferred_element_type=jnp.float32
        )
    flux_grid = flux_grid.astype(jnp.bfloat16)

    latitude = jnp.sin(
        math.pi * (lat_of_row.astype(jnp.float32) + 0.5) / (lat_dev * owners) - math.pi / 2
    )
    regridded = 0.0
    for index in range(len(chunks) - fused):
        regridded += lax.dot_general(
            returned[index].reshape(-1, cells),
            tables[index],
            (((0,), (0,)), ((), ())),
            preferred_element_type=jnp.float32,
        )
    if fused:
        regridded = jnp.broadcast_to(regridded, rows_flat.shape).astype(jnp.bfloat16)
        regridded = lax.optimization_barrier(regridded)
        atm_out = final_call(
            returned[-1].reshape(-1, cells), tables[-1], regridded, rows_flat, latitude
        )
    else:
        latitude = jnp.broadcast_to(latitude[None], (lev_dev, lat_dev)).reshape(cells, 1)
        atm_out = regridded * (1.0 + rows_flat.astype(jnp.float32) * latitude)
    atm_out = atm_out.astype(jnp.bfloat16).reshape(lev_dev, lat_dev, lon_count)

    ocean_now = ocean(ocean_temp, diffusivity, surface_heat, land_mask)

    ocean_rows, ocean_cols = diffusivity.shape
    pieces = lon_count // ocean_cols
    segments = flux_grid.reshape(lat_dev * pieces, ocean_cols)
    pairs_dev = remap_mats.shape[1]
    all_dest = pair_dest[0, :, 0].reshape(owners, pairs_dev)
    all_dst = pair_dst[0].reshape(owners, pairs_dev)
    earlier = jnp.arange(pairs_dev)[None, :] < jnp.arange(pairs_dev)[:, None]
    rank = jnp.sum(
        (all_dest[:, :, None] == all_dest[:, None, :]) & earlier[None], axis=2, dtype=jnp.int32
    )
    my_src = lax.dynamic_slice_in_dim(pair_src[0], my_owner * pairs_dev, pairs_dev)
    chosen = jnp.take(segments, my_src, axis=0)
    products = jnp.einsum("pij,pj->pi", remap_mats[0], chosen, preferred_element_type=jnp.float32)
    place = lax.dynamic_index_in_dim(all_dest * CAP + rank, my_owner, 0, keepdims=False)
    outgoing = jnp.dot(
        (jnp.arange(owners * CAP, dtype=jnp.int32)[:, None] == place[None, :]).astype(jnp.float32),
        products,
        precision=lax.Precision.HIGHEST,
        preferred_element_type=jnp.float32,
    )
    outgoing = outgoing.reshape(owners, CAP, ocean_cols)
    incoming = share_pairs(outgoing)
    mine = (all_dest == my_owner)[:, None, :] & (
        rank[:, None, :] == jnp.arange(CAP, dtype=jnp.int32)[None, :, None]
    )
    row_hit = all_dst[None, :, None, :] == jnp.arange(ocean_rows, dtype=jnp.int32)[:, None, None, None]
    picker = jnp.any(mine[None] & row_hit, axis=3).astype(jnp.float32)
    ocean_flux = jnp.dot(
        picker.reshape(ocean_rows, owners * CAP),
        incoming.reshape(owners * CAP, ocean_cols),
        precision=lax.Precision.HIGHEST,
        preferred_element_type=jnp.float32,
    )
    return (atm_out, ocean_now, ocean_flux)


def solution(mesh):
    return jax.shard_map(
        per_device,
        mesh=mesh,
        in_specs=(
            P("lev", "wav", None),
            P("wav", None, None),
            P(),
            P("wav"),
            P(),
            P(),
            P(),
            P(),
            P("lev", "wav", None, None),
            P("lev", None, None),
            P("lev", None),
            P("lev", None),
            P(None, "lev", "wav"),
            P("lev", "wav"),
            P("lev", "wav"),
            P("lev", "wav"),
        ),
        out_specs=(P("lev", "wav", None), P(None, "lev", "wav"), P("lev", "wav")),
        check_vma=False,
    )
```

```python
import functools
import math

import jax
import jax.numpy as jnp
from jax import lax
from jax.experimental import pallas as pl
from jax.experimental.pallas import tpu as pltpu
from jax.sharding import PartitionSpec as P


SWEEPS = 4
CAP = 2
AXES = ("lev", "wav")
CHUNKS = (2, 3)
UNIT = 4
BLOCK = 1280
LANES = 128


def with_halo(value, sides, width):
    for axis, dim in sides:
        count, length = (lax.axis_size(axis), value.shape[dim])
        up = [(i, (i + 1) % count) for i in range(count - 1)]
        down = [(j, i) for i, j in up]
        last = lax.slice_in_dim(value, length - width, length, axis=dim)
        initial = lax.slice_in_dim(value, 0, width, axis=dim)
        before = lax.ppermute(last, axis, up)
        after = lax.ppermute(initial, axis, down)
        value = jnp.concatenate([before, value, after], axis=dim)
    return value


def exchange(value):
    return lax.all_to_all(value, AXES, split_axis=0, concat_axis=0, tiled=True)


def table_kernel(unit, lon_count, waves_ref, table_ref):
    rows = waves_ref.shape[0]
    lane = lax.broadcasted_iota(jnp.int32, (rows, LANES), 1)
    half = (lax.broadcasted_iota(jnp.int32, (rows, LANES), 0) // unit) % 2
    waves = jnp.broadcast_to(waves_ref[...], (rows, LANES))
    scale = jnp.where(waves < 0, 0.0, math.sqrt(2.0 / lon_count))

    def angle(steps):
        steps = steps.astype(jnp.float32)
        steps = steps - lon_count * jnp.round(steps * (1.0 / lon_count))
        return steps * (2.0 * math.pi / lon_count)

    low = angle(waves * lane + half * (lon_count // 4))
    high = angle(waves * (lane * LANES))
    cos_low, sin_low = scale * jnp.cos(low), scale * jnp.sin(low)
    cos_high, sin_high = jnp.cos(high), jnp.sin(high)
    for tile in range(lon_count // LANES):
        part = cos_low * cos_high[:, tile : tile + 1] - sin_low * sin_high[:, tile : tile + 1]
        table_ref[:, tile * LANES : (tile + 1) * LANES] = part.astype(jnp.bfloat16)


def swap(value, axis, bit, place):
    pairs = [(i, i ^ bit) for i in range(lax.axis_size(axis))]
    mine = (lax.axis_index(axis) // bit) % 2
    if place is None:
        kept = sent = value
        place = 1
    else:
        kept = lax.dynamic_index_in_dim(value, mine, place, keepdims=False)
        sent = lax.dynamic_index_in_dim(value, 1 - mine, place, keepdims=False)
    came = lax.ppermute(sent, axis, pairs)
    first = jnp.where(mine == 0, kept, came)
    second = jnp.where(mine == 0, came, kept)
    return jnp.stack([first, second], axis=place)


def bits_of(axis):
    return [1 << i for i in range(lax.axis_size(axis).bit_length() - 1)]


def power_of_two(axis):
    return lax.axis_size(axis) & (lax.axis_size(axis) - 1) == 0


def share_flux(value):
    owners, columns, rows = value.shape
    groups = lax.axis_size("lev")
    if not (power_of_two("lev") and power_of_two("wav")):
        copies = jnp.broadcast_to(value[None], (groups,) + value.shape)
        return exchange(copies.reshape(groups * owners, columns, rows))
    for bit in bits_of("lev"):
        value = swap(value, "lev", bit, None)
    bits = bits_of("wav")
    value = value.reshape((2,) * len(bits) + (groups, columns, rows))
    for index, bit in enumerate(bits):
        value = swap(value, "wav", bit, len(bits) - 1 - index)
    value = value.reshape(owners, groups, columns, rows).transpose(1, 0, 2, 3)
    return value.reshape(groups * owners, columns, rows)


def share_pairs(value):
    if not power_of_two("wav"):
        return lax.all_to_all(value, "wav", split_axis=0, concat_axis=0, tiled=True)
    bits = bits_of("wav")
    shape = value.shape
    value = value.reshape((2,) * len(bits) + shape[1:])
    for index, bit in enumerate(bits):
        value = swap(value, "wav", bit, len(bits) - 1 - index)
    return value.reshape(shape)


def wave_table(waves, valid, unit, lon_count):
    devices, count = waves.shape
    waves = jnp.where(valid, waves, -1).reshape(devices, count // unit, 1, unit)
    waves = jnp.broadcast_to(waves, (devices, count // unit, 2, unit)).reshape(-1, 1)
    rows = waves.shape[0]
    block = math.gcd(rows, 128)
    if block % (2 * unit):
        block = rows
    return pl.pallas_call(
        functools.partial(table_kernel, unit, lon_count),
        grid=(rows // block,),
        in_specs=[pl.BlockSpec((block, 1), lambda i: (i, 0))],
        out_specs=pl.BlockSpec((block, lon_count), lambda i: (i, 0)),
        out_shape=jax.ShapeDtypeStruct((rows, lon_count), jnp.bfloat16),
    )(waves)


def fourier_kernel(
    owners, slots_owner, slots_dev, start, units, waves_ref, rows_ref, fourier_ref, table_ref
):
    rows, lon_count = table_ref.shape
    tile_rows = 2 * UNIT

    @pl.when(pl.program_id(0) == 0)
    def _():
        lane = lax.broadcasted_iota(jnp.int32, (tile_rows, LANES), 1)
        row = lax.broadcasted_iota(jnp.int32, (tile_rows, LANES), 0)
        upper = row < UNIT
        first = lane == 0
        scale = math.sqrt(2.0 / lon_count)

        def tile(index, carry):
            waves = jnp.zeros((tile_rows, LANES), jnp.int32)
            for part in range(2):
                group = index * 2 + part
                device = group // units
                slot = (device % owners) * slots_owner + (device // owners) * slots_dev
                slot = slot + start + group % units * UNIT
                for i in range(UNIT):
                    waves = jnp.where(row == part * UNIT + i, waves_ref[slot + i], waves)
            steps = jnp.where(first, waves * LANES, waves * lane).astype(jnp.float32)
            steps = steps - lon_count * jnp.round(steps * (1.0 / lon_count))
            angle = steps * (2.0 * math.pi / lon_count)
            cosine, sine = jnp.cos(angle), jnp.sin(angle)
            cos_step = jnp.broadcast_to(cosine[:, :1], cosine.shape)
            sin_step = jnp.broadcast_to(sine[:, :1], sine.shape)
            cosine = scale * jnp.where(first, 1.0, cosine)
            sine = -scale * jnp.where(first, 0.0, sine)
            place = pl.ds(pl.multiple_of(index * 2 * tile_rows, 2 * tile_rows), 2 * tile_rows)
            for column in range(lon_count // LANES):
                pair = [
                    jnp.where(upper, cosine, pltpu.roll(sine, UNIT, 0)),
                    jnp.where(upper, pltpu.roll(cosine, UNIT, 0), sine),
                ]
                table_ref[place, column * LANES : (column + 1) * LANES] = jnp.concatenate(
                    pair, axis=0
                ).astype(jnp.bfloat16)
                cosine, sine = (
                    cosine * cos_step + sine * sin_step,
                    sine * cos_step - cosine * sin_step,
                )
            return carry

        tiles = rows // (2 * tile_rows)
        lax.fori_loop(0, tiles, tile, 0, unroll=math.gcd(tiles, 16))

    fourier_ref[...] = lax.dot_general(
        table_ref[...], rows_ref[...], (((1,), (1,)), ((), ())), preferred_element_type=jnp.float32
    ).astype(jnp.bfloat16)


def fourier_call(waves, rows_flat, owners, devices, slots_owner, slots_dev, start, count):
    cells, lon_count = rows_flat.shape
    rows = devices * 2 * count
    block = math.gcd(cells, BLOCK)
    body = functools.partial(
        fourier_kernel, owners, slots_owner, slots_dev, start, count // UNIT
    )
    return pl.pallas_call(
        body,
        grid_spec=pltpu.PrefetchScalarGridSpec(
            num_scalar_prefetch=1,
            grid=(cells // block,),
            in_specs=[pl.BlockSpec((block, lon_count), lambda i, waves: (i, 0))],
            out_specs=[
                pl.BlockSpec((rows, block), lambda i, waves: (0, i)),
                pl.BlockSpec((rows, lon_count), lambda i, waves: (0, 0)),
            ],
        ),
        out_shape=[
            pltpu.HBM((rows, cells), jnp.bfloat16),
            pltpu.HBM((rows, lon_count), jnp.bfloat16),
        ],
        compiler_params=pltpu.CompilerParams(vmem_limit_bytes=32 * 1024 * 1024),
    )(
        pltpu.with_memory_space_constraint(waves, pltpu.HBM),
        pltpu.with_memory_space_constraint(rows_flat, pltpu.HBM),
    )


def final_kernel(lat_dev, returned_ref, table_ref, partial_ref, rows_ref, latitude_ref, out_ref):
    total = partial_ref[...].astype(jnp.float32) + lax.dot_general(
        returned_ref[...],
        table_ref[...],
        (((0,), (0,)), ((), ())),
        preferred_element_type=jnp.float32,
    )
    shape = (out_ref.shape[0] // lat_dev, lat_dev, out_ref.shape[1])
    field = rows_ref[...].astype(jnp.float32).reshape(shape)
    total = total.reshape(shape) * (1.0 + field * latitude_ref[...][None])
    out_ref[...] = total.reshape(out_ref.shape).astype(jnp.bfloat16)


def final_call(returned, table, partial, rows_flat, latitude):
    cells, lon_count = rows_flat.shape
    lat_dev = latitude.shape[0]
    columns = returned.shape[0]
    block = lat_dev * 16
    rows = pl.BlockSpec((block, lon_count), lambda i: (i, 0))
    return pl.pallas_call(
        functools.partial(final_kernel, lat_dev),
        grid=(cells // block,),
        in_specs=[
            pl.BlockSpec((columns, block), lambda i: (0, i)),
            pl.BlockSpec((columns, lon_count), lambda i: (0, 0)),
            rows,
            rows,
            pl.BlockSpec((lat_dev, 1), lambda i: (0, 0)),
        ],
        out_specs=rows,
        out_shape=pltpu.HBM((cells, lon_count), jnp.bfloat16),
        compiler_params=pltpu.CompilerParams(vmem_limit_bytes=32 * 1024 * 1024),
    )(
        pltpu.with_memory_space_constraint(returned, pltpu.HBM),
        table,
        pltpu.with_memory_space_constraint(partial, pltpu.HBM),
        pltpu.with_memory_space_constraint(rows_flat, pltpu.HBM),
        latitude[:, None],
    )


def segments(length, source, target):
    cuts = {0}
    cuts.update(i for i in range(1, length) if (source + i) % LANES == 0)
    cuts.update(i for i in range(1, length) if (target + i) % LANES == 0)
    return [
        ((source + i) // LANES, (target + i) // LANES, (target + i) % LANES) for i in sorted(cuts)
    ]


def move_runs(load, store, lane, runs):
    tile, value = 0, None
    for index, source, target, length in runs:
        for src, dst, low in segments(length, source, target):
            piece = pltpu.roll(load(index, src), (target - source) % LANES, 1) if (
                target - source
            ) % LANES else load(index, src)
            if dst != tile:
                store(tile, value)
                tile, value = dst, None
            value = piece if low == 0 else jnp.where(lane >= low, piece, value)
    store(tile, value)


def spectral_kernel(
    groups,
    owners,
    lev_dev,
    lat_dev,
    base_ref,
    waves_ref,
    arrived_ref,
    leg_ref,
    analysis_ref,
    synthesis_ref,
    damping_ref,
    weights_ref,
    sent_ref,
    flux_ref,
    stage_ref,
):
    rows = 2 * UNIT
    levels = groups * lev_dev
    wave_count = leg_ref.shape[2]
    width = owners * lat_dev
    unit = pl.program_id(0)
    lane = lax.broadcasted_iota(jnp.int32, (rows, LANES), 1)

    def take(group, carry):
        for x in range(lev_dev):
            first = pl.multiple_of((group * lev_dev + x) * rows, rows)

            def load(owner, tile):
                part = arrived_ref[group * owners + owner, :, tile * LANES : (tile + 1) * LANES]
                return part.astype(jnp.float32)

            def store(tile, value):
                stage_ref[tile, pl.ds(first, rows), :] = value

            move_runs(
                load,
                store,
                lane,
                [(w, x * lat_dev, w * lat_dev, lat_dev) for w in range(owners)],
            )
        return carry

    lax.fori_loop(0, groups, take, 0)
    degree = lax.broadcasted_iota(jnp.int32, (2 * levels, wave_count), 1)
    flux_row = lax.broadcasted_iota(jnp.int32, (16, wave_count), 0)

    def solve(slot, carry):
        halves = [
            [
                stage_ref[tile, pl.ds(k * UNIT + slot, levels, stride=rows), :]
                for tile in range(width // LANES)
            ]
            for k in range(2)
        ]
        fields = jnp.concatenate([jnp.concatenate(half, axis=1) for half in halves], axis=0)
        leg = leg_ref[slot]
        spectra = jnp.dot(fields.astype(jnp.bfloat16), leg, preferred_element_type=jnp.float32)
        wave = waves_ref[unit * UNIT + slot]
        spectra = jnp.where(degree >= wave, spectra, 0.0).astype(jnp.bfloat16)
        solved, flux = [], 0.0
        for k in range(2):
            modal = jnp.dot(
                analysis_ref[...],
                spectra[k * levels : (k + 1) * levels],
                preferred_element_type=jnp.float32,
            )
            modal = (modal * damping_ref[...]).astype(jnp.bfloat16)
            part = jnp.dot(
                synthesis_ref[...], modal, preferred_element_type=jnp.float32
            ).astype(jnp.bfloat16)
            coef = jnp.sum(weights_ref[...] * part.astype(jnp.float32), axis=0, keepdims=True)
            flux = jnp.where(flux_row == k, coef, flux)
            solved.append(part)
        solved.append(flux.astype(jnp.bfloat16))
        grid = lax.dot_general(
            jnp.concatenate(solved, axis=0),
            leg,
            (((1,), (1,)), ((), ())),
            preferred_element_type=jnp.float32,
        )
        for k in range(2):
            for tile in range(width // LANES):
                stage_ref[tile, pl.ds(k * UNIT + slot, levels, stride=rows), :] = grid[
                    k * levels : (k + 1) * levels, tile * LANES : (tile + 1) * LANES
                ]
            flux_ref[0, pl.ds(k * UNIT + slot, 1), :] = grid[2 * levels + k : 2 * levels + k + 1]
        return carry

    lax.fori_loop(0, UNIT, solve, 0)

    def send(group, carry):
        for w in range(owners):

            def load(x, tile):
                first = pl.multiple_of((group * lev_dev + x) * rows, rows)
                return stage_ref[tile, pl.ds(first, rows), :]

            def store(tile, value):
                sent_ref[group * owners + w, :, tile * LANES : (tile + 1) * LANES] = value.astype(
                    jnp.bfloat16
                )

            move_runs(
                load,
                store,
                lane,
                [(x, w * lat_dev, x * lat_dev, lat_dev) for x in range(lev_dev)],
            )
        return carry

    lax.fori_loop(0, groups, send, 0)


def spectral_call(
    arrived,
    legendre,
    base,
    waves,
    analysis,
    synthesis,
    damping,
    weights,
    groups,
    owners,
    lev_dev,
    lat_dev,
):
    devices, columns, cells = arrived.shape
    units = columns // (2 * UNIT)
    levels = groups * lev_dev
    rows_all, wave_count = legendre.shape[1:]
    body = functools.partial(spectral_kernel, groups, owners, lev_dev, lat_dev)
    whole = lambda shape: pl.BlockSpec(shape, lambda i, base, waves: (0,) * len(shape))
    return pl.pallas_call(
        body,
        grid_spec=pltpu.PrefetchScalarGridSpec(
            num_scalar_prefetch=2,
            grid=(units,),
            in_specs=[
                pl.BlockSpec((devices, 2 * UNIT, cells), lambda i, base, waves: (0, i, 0)),
                pl.BlockSpec(
                    (UNIT, rows_all, wave_count), lambda i, base, waves: (base[0] + i, 0, 0)
                ),
                whole(analysis.shape),
                whole(synthesis.shape),
                whole(damping.shape),
                whole((levels, 1)),
            ],
            out_specs=[
                pl.BlockSpec((devices, 2 * UNIT, cells), lambda i, base, waves: (0, i, 0)),
                pl.BlockSpec((1, 2 * UNIT, rows_all), lambda i, base, waves: (i, 0, 0)),
            ],
            scratch_shapes=[
                pltpu.VMEM((rows_all // LANES, levels * 2 * UNIT, LANES), jnp.float32)
            ],
        ),
        out_shape=[
            pltpu.HBM(arrived.shape, jnp.bfloat16),
            jax.ShapeDtypeStruct((units, 2 * UNIT, rows_all), jnp.float32),
        ],
        compiler_params=pltpu.CompilerParams(vmem_limit_bytes=48 * 1024 * 1024),
    )(base, waves, arrived, legendre, analysis, synthesis, damping, weights.reshape(levels, 1))


def split_slots(count, unit):
    total = sum(CHUNKS) * unit
    if count % total:
        return [(0, count)]
    start, out = 0, []
    for part in CHUNKS:
        part = count // sum(CHUNKS) * part
        out.append((start, part))
        start += part
    return out


def ocean(ocean_temp, diffusivity, surface_heat, land_mask):
    ocean_levels = ocean_temp.shape[0]
    ocean_mask = land_mask.astype(jnp.float32)
    level_one = (jnp.arange(ocean_levels, dtype=jnp.int32) == 0).astype(jnp.float32)[:, None, None]
    ocean_now = ocean_temp * ocean_mask[None]
    stacked = jnp.concatenate(
        [ocean_now, ocean_mask[None], diffusivity[None], surface_heat[None]], axis=0
    )
    padded = with_halo(stacked.astype(jnp.bfloat16), (("lev", 1), ("wav", 2)), SWEEPS).astype(
        stacked.dtype
    )
    current = padded[:ocean_levels]
    for sweep_idx in range(SWEEPS):
        margin = sweep_idx + 1
        inside = current[:, 1:-1, 1:-1]
        laplace = (
            current[:, 2:, 1:-1]
            + current[:, :-2, 1:-1]
            + current[:, 1:-1, 2:]
            + current[:, 1:-1, :-2]
            - 4.0 * inside
        )
        mask_in = padded[ocean_levels, margin:-margin, margin:-margin]
        kappa_in = padded[ocean_levels + 1, margin:-margin, margin:-margin]
        heat_in = padded[ocean_levels + 2, margin:-margin, margin:-margin]
        current = mask_in[None] * (inside + kappa_in[None] * laplace + level_one * heat_in[None])
    return current


def per_device(
    grid_field,
    legendre,
    wave_of_slot,
    lat_of_row,
    analysis,
    synthesis,
    mode_rates,
    flux_weights,
    remap_mats,
    pair_dest,
    pair_src,
    pair_dst,
    ocean_temp,
    diffusivity,
    surface_heat,
    land_mask,
):
    groups = lax.axis_size("lev")
    owners = lax.axis_size("wav")
    devices = groups * owners
    my_group = lax.axis_index("lev")
    my_owner = lax.axis_index("wav")
    lev_dev, lat_dev, lon_count = grid_field.shape
    wave_count = wave_of_slot.shape[0]
    slots_owner = wave_count // owners
    slots_dev = -(-slots_owner // groups)
    cells = lev_dev * lat_dev
    rows_flat = grid_field.reshape(cells, lon_count)
    degree = jnp.arange(wave_count, dtype=jnp.int32)
    damp_base = (degree * (degree + 1)).astype(jnp.float32) / float(wave_count * wave_count)
    damping = 1.0 / (1.0 + mode_rates[:, None] * damp_base[None, :])

    def slots_of(group, owner, start, count):
        local = group * slots_dev + start + jnp.arange(count, dtype=jnp.int32)
        slot = owner * slots_owner + jnp.minimum(local, slots_owner - 1)
        return local, wave_of_slot[slot], local < slots_owner

    exact = slots_owner == slots_dev * groups
    fused = (
        exact
        and slots_dev % UNIT == 0
        and lon_count % LANES == 0
        and cells % LANES == 0
        and owners * lat_dev % LANES == 0
        and groups * lev_dev % 8 == 0
        and lev_dev % 16 == 0
        and lat_dev % 16 == 0
    )
    unit = UNIT if fused else slots_dev
    chunks = split_slots(slots_dev, unit)
    spare = groups * slots_dev - slots_owner
    all_waves = jnp.pad(wave_of_slot.reshape(owners, slots_owner), ((0, 0), (0, spare)))
    all_waves = all_waves.reshape(owners, groups, slots_dev).transpose(1, 0, 2)
    all_valid = jnp.arange(groups * slots_dev, dtype=jnp.int32) < slots_owner
    all_valid = jnp.broadcast_to(all_valid.reshape(groups, 1, slots_dev), all_waves.shape)
    all_waves = all_waves.reshape(devices, slots_dev)
    all_valid = all_valid.reshape(devices, slots_dev)

    def forward(start, count):
        if fused:
            fourier, table = fourier_call(
                wave_of_slot, rows_flat, owners, devices, slots_owner, slots_dev, start, count
            )
            return table, fourier.reshape(devices, 2 * count, cells)
        chosen = slice(start, start + count)
        table = wave_table(all_waves[:, chosen], all_valid[:, chosen], unit, lon_count)
        fourier = lax.dot_general(
            table, rows_flat, (((1,), (1,)), ((), ())), preferred_element_type=jnp.float32
        ).astype(jnp.bfloat16)
        return table, fourier.reshape(devices, 2 * count, cells)

    def spectral_fused(arrived, start, count):
        base = my_group * (slots_dev // UNIT) + start // UNIT
        first = my_owner * slots_owner + my_group * slots_dev + start
        my_waves = lax.dynamic_slice_in_dim(wave_of_slot, first, count)
        grid_coef, flux_lat = spectral_call(
            arrived,
            legendre,
            base.astype(jnp.int32).reshape(1),
            my_waves,
            analysis,
            synthesis,
            damping,
            flux_weights,
            groups,
            owners,
            lev_dev,
            lat_dev,
        )
        return grid_coef, flux_lat.astype(jnp.bfloat16).reshape(2 * count, owners, lat_dev)

    def spectral(arrived, start, count):
        arrived, my_analysis, my_synthesis, my_damping, my_weights = lax.optimization_barrier(
            (arrived, analysis, synthesis, damping, flux_weights)
        )
        local, my_waves, _ = slots_of(my_group, my_owner, start, count)
        if exact:
            leg = lax.dynamic_slice_in_dim(legendre, my_group * slots_dev + start, count, axis=0)
        else:
            leg = jnp.take(legendre, jnp.minimum(local, slots_owner - 1), axis=0)
        fields = arrived.reshape(groups, owners, 2, count, lev_dev, lat_dev)
        fields = fields.transpose(3, 1, 2, 0, 4, 5).reshape(
            count, owners, 2 * groups * lev_dev, lat_dev
        )
        leg_rows = leg.reshape(count, owners, lat_dev, wave_count)
        spectra = jnp.einsum(
            "swmr,swrn->smn", fields, leg_rows, preferred_element_type=jnp.float32
        ).reshape(count, 2, groups * lev_dev, wave_count)
        retained = degree[None, :] >= my_waves[:, None]
        spectra = jnp.where(retained[:, None, None, :], spectra, 0.0).astype(jnp.bfloat16)
        modal_coef = jnp.einsum(
            "ix,skxn->skin", my_analysis, spectra, preferred_element_type=jnp.float32
        )
        modal_coef = (modal_coef * my_damping[None, None]).astype(jnp.bfloat16)
        solved = jnp.einsum(
            "xi,skin->skxn", my_synthesis, modal_coef, preferred_element_type=jnp.float32
        ).astype(jnp.bfloat16)
        flux_coef = jnp.sum(
            my_weights[None, None, :, None] * solved.astype(jnp.float32), axis=2
        ).astype(jnp.bfloat16)
        grid_coef = jnp.einsum(
            "smn,swrn->swmr",
            solved.reshape(count, 2 * groups * lev_dev, wave_count),
            leg_rows,
            preferred_element_type=jnp.float32,
        ).astype(jnp.bfloat16)
        grid_coef = grid_coef.reshape(count, owners, 2, groups, lev_dev, lat_dev)
        grid_coef = grid_coef.transpose(3, 1, 2, 0, 4, 5).reshape(devices, 2 * count, cells)
        flux_lat = lax.dot_general(
            flux_coef, leg, (((2,), (2,)), ((0,), (0,))), preferred_element_type=jnp.float32
        ).astype(jnp.bfloat16)
        flux_lat = flux_lat.reshape(count, 2, owners, lat_dev).transpose(1, 0, 2, 3)
        return grid_coef, flux_lat.reshape(2 * count, owners, lat_dev)

    tables, arrivals, returned, sent, flux_parts = [], [], [], [], []
    for chunk in chunks:
        table, fourier = forward(*chunk)
        tables.append(table)
        arrivals.append(exchange(fourier))
    for index, chunk in enumerate(chunks):
        step = spectral_fused if fused else spectral
        grid_coef, flux_lat = step(arrivals[index], *chunk)
        sent.append(grid_coef)
        flux_parts.append(flux_lat)
    for value in sent:
        returned.append(exchange(value))
    flux_lat = jnp.concatenate(flux_parts, axis=0).transpose(1, 0, 2)
    flux_back = share_flux(flux_lat)

    flux_grid = 0.0
    for (start, count), table in zip(chunks, tables):
        part = flux_back[:, 2 * start : 2 * (start + count)].reshape(-1, lat_dev)
        flux_grid += lax.dot_general(
            part, table, (((0,), (0,)), ((), ())), preferred_element_type=jnp.float32
        )
    flux_grid = flux_grid.astype(jnp.bfloat16)

    latitude = jnp.sin(
        math.pi * (lat_of_row.astype(jnp.float32) + 0.5) / (lat_dev * owners) - math.pi / 2
    )
    regridded = 0.0
    for index in range(len(chunks) - fused):
        regridded += lax.dot_general(
            returned[index].reshape(-1, cells),
            tables[index],
            (((0,), (0,)), ((), ())),
            preferred_element_type=jnp.float32,
        )
    if fused:
        regridded = jnp.broadcast_to(regridded, rows_flat.shape).astype(jnp.bfloat16)
        regridded = lax.optimization_barrier(regridded)
        atm_out = final_call(
            returned[-1].reshape(-1, cells), tables[-1], regridded, rows_flat, latitude
        )
    else:
        latitude = jnp.broadcast_to(latitude[None], (lev_dev, lat_dev)).reshape(cells, 1)
        atm_out = regridded * (1.0 + rows_flat.astype(jnp.float32) * latitude)
    atm_out = atm_out.astype(jnp.bfloat16).reshape(lev_dev, lat_dev, lon_count)

    ocean_now = ocean(ocean_temp, diffusivity, surface_heat, land_mask)

    ocean_rows, ocean_cols = diffusivity.shape
    pieces = lon_count // ocean_cols
    segments = flux_grid.reshape(lat_dev * pieces, ocean_cols)
    pairs_dev = remap_mats.shape[1]
    all_dest = pair_dest[0, :, 0].reshape(owners, pairs_dev)
    all_dst = pair_dst[0].reshape(owners, pairs_dev)
    earlier = jnp.arange(pairs_dev)[None, :] < jnp.arange(pairs_dev)[:, None]
    rank = jnp.sum(
        (all_dest[:, :, None] == all_dest[:, None, :]) & earlier[None], axis=2, dtype=jnp.int32
    )
    my_src = lax.dynamic_slice_in_dim(pair_src[0], my_owner * pairs_dev, pairs_dev)
    chosen = jnp.take(segments, my_src, axis=0)
    products = jnp.einsum("pij,pj->pi", remap_mats[0], chosen, preferred_element_type=jnp.float32)
    place = lax.dynamic_index_in_dim(all_dest * CAP + rank, my_owner, 0, keepdims=False)
    outgoing = jnp.dot(
        (jnp.arange(owners * CAP, dtype=jnp.int32)[:, None] == place[None, :]).astype(jnp.float32),
        products,
        precision=lax.Precision.HIGHEST,
        preferred_element_type=jnp.float32,
    )
    outgoing = outgoing.reshape(owners, CAP, ocean_cols)
    incoming = share_pairs(outgoing)
    mine = (all_dest == my_owner)[:, None, :] & (
        rank[:, None, :] == jnp.arange(CAP, dtype=jnp.int32)[None, :, None]
    )
    row_hit = all_dst[None, :, None, :] == jnp.arange(ocean_rows, dtype=jnp.int32)[:, None, None, None]
    picker = jnp.any(mine[None] & row_hit, axis=3).astype(jnp.float32)
    ocean_flux = jnp.dot(
        picker.reshape(ocean_rows, owners * CAP),
        incoming.reshape(owners * CAP, ocean_cols),
        precision=lax.Precision.HIGHEST,
        preferred_element_type=jnp.float32,
    )
    return (atm_out, ocean_now, ocean_flux)


def solution(mesh):
    return jax.shard_map(
        per_device,
        mesh=mesh,
        in_specs=(
            P("lev", "wav", None),
            P("wav", None, None),
            P(),
            P("wav"),
            P(),
            P(),
            P(),
            P(),
            P("lev", "wav", None, None),
            P("lev", None, None),
            P("lev", None),
            P("lev", None),
            P(None, "lev", "wav"),
            P("lev", "wav"),
            P("lev", "wav"),
            P("lev", "wav"),
        ),
        out_specs=(P("lev", "wav", None), P(None, "lev", "wav"), P("lev", "wav")),
        check_vma=False,
    )
```
